256 devices in a mesh: video: 4 (over x), tm: 16 (over z, core), space: 4 (over y).
Axes of the slice: x: 4, y: 4, z: 8, core: 2. Of those that a mesh axis runs over, the one named last changes fastest.
Arguments:
- feature_maps: bfloat16 [64, 128, 240, 128], P(('video', 'tm'), 'space'), parts along dimension 0, may hold values from -27 to 27
- query_frame: int32 [2048], P('video'), parts along dimension 0, may hold values from 0 to 15
- query_row: int32 [2048], P('video'), parts along dimension 0, may hold values from 0 to 127
- query_col: int32 [2048], P('video'), parts along dimension 0, may hold values from 0 to 239
- ema_decay: float32 [64, 128], P(('video', 'tm')), parts along dimension 0, may hold values from 0.14 to 1
- dw_kernel: float32 [3, 128], replicated, may hold values from -3 to 3
- pw_weight: bfloat16 [128, 128], replicated, may hold values from -0.5 to 0.5
- out_weight: float32 [2, 128], replicated, may hold values from -2 to 2
Outputs:
- tracks: float32 [64, 2, 512], P(('video', 'tm')), parts along dimension 0
The draws below stay inside these ranges and needn't reach their ends.
There are 4 independent parts, one for each index of `video`. The reference program is written for one: setup_inputs(seed, part) draws one part's arguments, and reference() takes and returns one part's arrays. A program takes and returns all parts, laid end to end along the dimension named above; an argument that names none is the same for every part. Nothing has to cross between parts.
All inputs are finite; a program needn't handle non-finite values.
Results may differ from the reference program's by a relative error of at most 0.0026.
Values may be sent and summed in bfloat16 or wider, within the bound.
A program may use at most 128 MiB of HBM per device.

```python
import math
import jax
import jax.numpy as jnp
import numpy as np
from jax import lax

CH = 128
WIDTH = 240
ROWS_DEV = 32
QUERIES = 512
KT = 3
HEIGHT = 128
CLIP_IMAGES = 16
N_SPACE = 4


def draw_feature_maps(key, part):
    base_values = jnp.clip(jax.random.normal(key, (CLIP_IMAGES, HEIGHT, WIDTH, CH), jnp.float32), -6.0, 6.0)
    return base_values.astype(jnp.bfloat16)


def draw_ema_decay(key, part):
    share = 0.5
    chooser = jax.random.uniform(jax.random.fold_in(key, 1), (1, CH), jnp.float32)
    slow_rate = jnp.exp(jax.random.uniform(jax.random.fold_in(key, 2), (1, CH), jnp.float32, math.log(0.1) / CLIP_IMAGES, -0.001))
    fast_rate = jax.random.uniform(jax.random.fold_in(key, 3), (1, CH), jnp.float32, 0.3, 0.85)
    reference_speed = jnp.where(chooser < share, slow_rate, fast_rate)
    arbitrary_shift = jax.random.uniform(jax.random.fold_in(key, 4), (CLIP_IMAGES, CH), jnp.float32, 0.97, 1.0)
    group_pick = jax.random.uniform(jax.random.fold_in(key, 5), (CLIP_IMAGES, 1), jnp.float32)
    group_length = jax.random.uniform(jax.random.fold_in(key, 6), (CLIP_IMAGES, 1), jnp.float32, 0.5, 0.8)
    image_group = jnp.where(group_pick < 3.0 / CLIP_IMAGES, group_length, 1.0)
    return reference_speed * arbitrary_shift * image_group


def place_ends(values, stream_key, low, largest):
    spot = [jax.random.randint(jax.random.fold_in(stream_key, axis), (), 0, length) for axis, length in enumerate(values.shape)]
    widest = values.shape.index(max(values.shape))
    next_to = spot[:widest] + [(spot[widest] + 1) % values.shape[widest]] + spot[widest + 1:]
    return values.at[tuple(spot)].set(low).at[tuple(next_to)].set(largest)


def cumulative_ranks(count, slope):
    loads = [(1 << 20) // math.isqrt(standing ** slope) + 1 for standing in range(1, count + 1)]
    width = 1 + sum(loads) // (1 << 30)
    return np.cumsum(np.array([max(1, weight // width) for weight in loads]))


def ranked_ids(rng, dims, amount, slope):
    table = cumulative_ranks(amount, slope)
    pick = jax.random.randint(jax.random.fold_in(rng, 1), dims, 0, int(table[amount - 1]))
    grade = jnp.searchsorted(jnp.asarray(table, jnp.int32), pick, side="right")
    return jax.random.permutation(jax.random.fold_in(rng, 2), amount)[grade].astype(jnp.int32)


def bell_draw(own_key, extent, scale, most, kind=jnp.bfloat16):
    result = jax.random.normal(own_key, extent, jnp.float32) * scale
    return jnp.minimum(jnp.maximum(result, -most), most).astype(kind)


def setup_inputs(seed: int = 0, part: int = 0) -> dict:
    key_list = jax.random.split(jax.random.key(seed), 9)
    own_keys = jax.random.split(jax.random.fold_in(key_list[8], part), 9)
    feature_maps = draw_feature_maps(jax.random.fold_in(jax.random.fold_in(key_list[8], part), 71), part)
    query_frame = place_ends(ranked_ids(own_keys[1], (QUERIES,), CLIP_IMAGES, 2), jax.random.fold_in(own_keys[1], 3), 0, CLIP_IMAGES - 1).astype(jnp.int32)
    query_row = place_ends(jax.random.randint(own_keys[2], (QUERIES,), 0, HEIGHT), jax.random.fold_in(own_keys[2], 1), 0, HEIGHT - 1).astype(jnp.int32)
    query_col = place_ends(jax.random.randint(own_keys[3], (QUERIES,), 0, WIDTH), jax.random.fold_in(own_keys[3], 1), 0, WIDTH - 1).astype(jnp.int32)
    ema_decay = draw_ema_decay(jax.random.fold_in(jax.random.fold_in(key_list[8], part), 71), part)
    dw_kernel = bell_draw(key_list[5], (KT, CH), 0.5, 3.0, jnp.float32)
    pw_weight = bell_draw(key_list[6], (CH, CH), CH ** -0.5, 0.5)
    out_weight = bell_draw(key_list[7], (2, CH), 0.3, 2.0, jnp.float32)
    return dict(feature_maps=feature_maps, query_frame=query_frame, query_row=query_row, query_col=query_col, ema_decay=ema_decay, dw_kernel=dw_kernel, pw_weight=pw_weight, out_weight=out_weight)


def reference(feature_maps, query_frame, query_row, query_col, ema_decay, dw_kernel, pw_weight, out_weight):
    query_feats = feature_maps[query_frame, query_row, query_col]
    scale = 1.0 / math.sqrt(CH)
    col_coord = jnp.arange(WIDTH, dtype=jnp.int32).astype(jnp.float32) / WIDTH
    row_blocks = (jnp.arange(HEIGHT, dtype=jnp.int32).astype(jnp.float32) / HEIGHT).reshape(N_SPACE, ROWS_DEV)

    def per_block(items):
        frame_map, block_rows = items
        scores = jnp.dot(query_feats, frame_map.T, preferred_element_type=jnp.float32) * scale
        highest = lax.optimization_barrier(jnp.max(scores, axis=1))
        weights_exp = jnp.exp(scores - highest[:, None])
        totals = lax.optimization_barrier(jnp.sum(weights_exp, axis=1))
        grid = weights_exp.reshape(QUERIES, ROWS_DEV, WIDTH)
        col_part = lax.optimization_barrier(jnp.sum(lax.optimization_barrier(jnp.sum(grid, axis=1)) * col_coord[None, :], axis=1))
        line_portion = lax.optimization_barrier(jnp.sum(lax.optimization_barrier(jnp.sum(grid, axis=2)) * block_rows[None, :], axis=1))
        pos_sum = jnp.stack([col_part, line_portion], 1)
        feat_sum = jnp.dot(weights_exp.astype(jnp.bfloat16), frame_map, preferred_element_type=jnp.float32)
        return (highest, totals, pos_sum, feat_sum)

    def per_frame(frame_map):
        blocks = frame_map.reshape(N_SPACE, ROWS_DEV * WIDTH, CH)
        highest, totals, pos_sum, feat_sum = lax.map(per_block, (blocks, row_blocks))
        top_value = lax.optimization_barrier(jnp.max(highest, axis=0))
        factor = jnp.exp(highest - top_value[None])
        grand_total = lax.optimization_barrier(jnp.sum(factor * totals, axis=0))
        position = lax.optimization_barrier(jnp.sum(factor[..., None] * pos_sum, axis=0)) / grand_total[:, None]
        focused_result = (lax.optimization_barrier(jnp.sum(factor[..., None] * feat_sum, axis=0)) / grand_total[:, None]).astype(jnp.bfloat16)
        return (position, focused_result)
    position, focused_result = lax.map(per_frame, feature_maps)
    padded = jnp.pad(focused_result.astype(jnp.float32), ((1, 1), (0, 0), (0, 0)))
    depth = jnp.zeros((CLIP_IMAGES, QUERIES, CH), jnp.float32)
    for tap in range(KT):
        depth = depth + dw_kernel[tap][None, None, :] * padded[tap:tap + CLIP_IMAGES]
    hidden = jax.nn.gelu(depth).astype(jnp.bfloat16)
    mixed = jnp.dot(hidden.reshape(-1, CH), pw_weight, preferred_element_type=jnp.float32).reshape(CLIP_IMAGES, QUERIES, CH)
    refined = focused_result.astype(jnp.float32) + mixed

    def ema_step(carried, items):
        retain, update = items
        carried = retain[None, :] * carried + (1.0 - retain[None, :]) * update
        return (carried, carried)
    start_state = jnp.zeros((QUERIES, CH), jnp.float32)
    final_state, memory = lax.scan(ema_step, start_state, (ema_decay, refined))
    delta = jnp.einsum('tqc,kc->tkq', memory, out_weight, precision=lax.Precision.HIGHEST)
    return jnp.transpose(position, (0, 2, 1)) + delta
```

```python
import functools
import math

import jax
import jax.numpy as jnp
from jax import lax
from jax.experimental import pallas as pl
from jax.experimental.pallas import tpu as pltpu
from jax.sharding import PartitionSpec as P

MESH = pl.DeviceIdType.MESH
F32 = jnp.float32
BF16 = jnp.bfloat16


def kernel(
    dims, fm, q_frame, q_row, q_col, decay, taps, pw, out_w, out,
    keys, keys32, keys_t, contrib32, contrib, rs_in, q_own, q_all, q_t, decay_all, tap_cols,
    pw_t, proj, scores, acc, part, part_in, att_own, att_in, term, term_in,
    key_sem, rs_send, rs_recv, ag_send, ag_recv, dec_send, dec_recv,
    part_send, part_recv, halo_send, halo_recv, term_send, term_recv,
):
    n_tm, n_sp, n_q, rows, width, ch, height = dims
    group = n_tm * n_sp
    per_home = n_q // group
    q_blk = n_q // n_sp
    n_pos = rows * width
    t = lax.axis_index("tm")
    y = lax.axis_index("space")
    me = y * n_tm + t

    def peer(r):
        other = lax.rem(me + r, group)
        return {"tm": lax.rem(other, n_tm), "space": lax.div(other, n_tm)}

    barrier = pltpu.get_barrier_semaphore()

    @pl.loop(1, group)
    def _(r):
        pl.semaphore_signal(barrier, inc=1, device_id=peer(r), device_id_type=MESH)

    load = pltpu.make_async_copy(fm, keys, key_sem)
    load.start()
    load.wait()

    step = 256

    @pl.loop(0, n_pos // step)
    def _(j):
        at = pl.multiple_of(j * step, step)
        keys32[pl.ds(at, step), :] = keys[pl.ds(at, step), :].astype(F32)

    keys32[pl.ds(n_pos, 8), :] = jnp.zeros((8, ch), F32)
    first_row = y * rows

    @pl.loop(0, n_q // 8)
    def _(i):
        for u in range(8):
            q = i * 8 + u
            row = q_row[q] - first_row
            mine = (q_frame[q] == t) & (row >= 0) & (row < rows)
            at = jnp.where(mine, row * width + q_col[q], n_pos)
            contrib32[pl.ds(q, 1), :] = keys32[pl.ds(at, 1), :]

    contrib[...] = contrib32[...].reshape(group, per_home, ch).astype(BF16)

    pl.semaphore_wait(barrier, group - 1)

    def rs_copy(r):
        other = lax.rem(me + r, group)
        return pltpu.make_async_remote_copy(
            contrib.at[other], rs_in.at[r - 1], rs_send, rs_recv,
            device_id=peer(r), device_id_type=MESH,
        )

    @pl.loop(1, group)
    def _(r):
        rs_copy(r).start()

    decay_all[t] = decay[...]

    @pl.loop(1, n_tm)
    def _(r):
        pltpu.make_async_remote_copy(
            decay, decay_all.at[t], dec_send, dec_recv,
            device_id={"tm": lax.rem(t + r, n_tm)}, device_id_type=MESH,
        ).start()

    @pl.loop(0, n_pos // 128)
    def _(j):
        at = pl.multiple_of(j * 128, 128)
        keys_t[pl.ds(0, ch), pl.ds(at, 128)] = keys32[pl.ds(at, 128), :].T.astype(BF16)

    place = lax.broadcasted_iota(jnp.int32, (16, n_pos), 1).astype(F32)
    line = jnp.floor((place + 0.5) * (1.0 / width))
    col = place - line * width
    line = line + (y * rows).astype(F32)
    kind = lax.broadcasted_iota(jnp.int32, (16, n_pos), 0)
    extra = jnp.where(kind == 0, 1.0, jnp.where(kind == 1, col, jnp.where(kind == 2, line, 0.0)))
    keys_t[pl.ds(ch, 16), :] = extra.astype(BF16)

    all_rs = pltpu.make_async_remote_copy(
        contrib.at[pl.ds(0, group - 1)], rs_in, rs_send, rs_recv,
        device_id=peer(1), device_id_type=MESH,
    )
    all_rs.wait_recv()
    total = contrib[me].astype(F32) + jnp.sum(rs_in[...].astype(F32), axis=0)
    q_own[...] = total.astype(BF16)
    q_all[me] = total.astype(BF16)

    @pl.loop(1, group)
    def _(r):
        pltpu.make_async_remote_copy(
            q_own, q_all.at[me], ag_send, ag_recv, device_id=peer(r), device_id_type=MESH
        ).start()

    eye = lax.broadcasted_iota(jnp.int32, (ch, ch), 0) == lax.broadcasted_iota(
        jnp.int32, (ch, ch), 1
    )
    for k in range(3):
        column = jnp.sum(jnp.where(eye, taps[pl.ds(k, 1), :], 0.0), axis=1, keepdims=True)
        tap_cols[k] = jnp.broadcast_to(column, (ch, q_blk))
    pw_t[...] = pw[...].astype(F32).T.astype(BF16)
    all_dec = pltpu.make_async_remote_copy(
        decay_all.at[pl.ds(0, n_tm - 1)], decay_all.at[pl.ds(0, n_tm - 1)], dec_send, dec_recv,
        device_id={"tm": lax.rem(t + 1, n_tm)}, device_id_type=MESH,
    )
    all_dec.wait()
    run = out_w[...] * (1.0 - decay[...])
    gain = jnp.zeros_like(run)
    for frame in range(n_tm):
        kept = gain if frame == 0 else gain * decay_all[frame]
        gain = jnp.where(t == frame, run, jnp.where(t < frame, kept, 0.0))
        proj[frame] = gain

    all_ag = pltpu.make_async_remote_copy(
        rs_in, rs_in, ag_send, ag_recv, device_id=peer(1), device_id_type=MESH
    )
    all_ag.wait_recv()
    q_t[...] = q_all[...].astype(F32).reshape(n_q, ch).T.astype(BF16)

    half = n_q // 2
    pair = lax.div(y, 2)
    scale = math.log2(math.e) / math.sqrt(ch)
    t1 = 768
    t2 = 1536

    def part_copy(slot, to):
        return pltpu.make_async_remote_copy(
            part.at[slot], part_in.at[slot - 1], part_send.at[slot - 1], part_recv.at[slot - 1],
            device_id={"space": to}, device_id_type=MESH,
        )

    for chunk in range(2):
        which = (1 - pair) if chunk == 0 else pair
        q_at = pl.multiple_of(which * half, half)

        def first(j, top):
            at = pl.multiple_of(j * t1, t1)
            s = jnp.dot(
                keys[pl.ds(at, t1), :], q_t[:, pl.ds(q_at, half)], preferred_element_type=F32
            )
            scores[pl.ds(at, t1), :] = s
            return jnp.maximum(top, jnp.max(s.reshape(t1 // 8, 8, half), axis=0))

        top = lax.fori_loop(0, n_pos // t1, first, jnp.full((8, half), -jnp.inf, F32))
        top = jnp.max(top, axis=0, keepdims=True)
        acc[...] = jnp.zeros_like(acc)

        @pl.loop(0, n_pos // t2)
        def _(j):
            at = pl.multiple_of(j * t2, t2)
            e = jnp.exp2((scores[pl.ds(at, t2), :] - top) * scale).astype(BF16)
            acc[...] += jnp.dot(keys_t[:, pl.ds(at, t2)], e, preferred_element_type=F32)

        for side in range(2):
            to = which * 2 + side
            slot = lax.rem(to - y + n_sp, n_sp)
            lanes = slice(side * q_blk, (side + 1) * q_blk)
            part[slot, pl.ds(0, ch + 8), :] = acc[pl.ds(0, ch + 8), lanes]
            part[slot, pl.ds(ch + 8, 8), :] = jnp.broadcast_to(top[:, lanes], (8, q_blk))
            if chunk == 0:
                part_copy(slot, to).start()
            else:

                @pl.when(slot != 0)
                def _():
                    part_copy(slot, to).start()

    for slot in range(1, n_sp):
        part_copy(slot, y).wait_recv()
    own = part[0]
    parts = [own] + [part_in[i] for i in range(n_sp - 1)]
    tops = [p[ch + 8 : ch + 9] for p in parts]
    best = functools.reduce(jnp.maximum, tops)
    mixed = None
    for p, m in zip(parts, tops):
        v = p[: ch + 8] * jnp.exp2((m - best) * scale)
        mixed = v if mixed is None else mixed + v
    inverse = 1.0 / mixed[ch : ch + 1]
    position = mixed[ch + 1 : ch + 3] * inverse
    unit = jnp.where(
        lax.broadcasted_iota(jnp.int32, (2, q_blk), 0) == 0, 1.0 / width, 1.0 / height
    )
    position = position * unit
    att = (mixed[:ch] * inverse).astype(BF16)
    att_own[...] = att

    def halo(side):
        to = lax.rem(t + (1 if side == 0 else n_tm - 1), n_tm)
        return pltpu.make_async_remote_copy(
            att_own, att_in.at[side], halo_send.at[side], halo_recv.at[side],
            device_id={"tm": to}, device_id_type=MESH,
        )

    halo(0).start()
    halo(1).start()
    att = att.astype(F32)
    mid = att * tap_cols[1]
    halo(0).wait_recv()
    halo(1).wait_recv()
    before = jnp.where(t > 0, att_in[0].astype(F32), 0.0)
    after = jnp.where(t < n_tm - 1, att_in[1].astype(F32), 0.0)
    depth = tap_cols[0] * before + mid + tap_cols[2] * after
    hidden = jax.nn.gelu(depth).astype(BF16)
    refined = att + jnp.dot(pw_t[...], hidden, preferred_element_type=F32)
    terms = jnp.dot(
        proj[...].reshape(2 * n_tm, ch), refined, preferred_element_type=F32,
        precision=lax.Precision.HIGHEST,
    )
    term[...] = terms.reshape(n_tm, 2, q_blk)
    term[t] = term[t] + position
    term_in[me] = term[t]

    @pl.loop(1, group)
    def _(r):
        other = peer(r)
        pltpu.make_async_remote_copy(
            term.at[other["tm"]], term_in.at[me], term_send, term_recv,
            device_id=other, device_id_type=MESH,
        ).start()

    all_term = pltpu.make_async_remote_copy(
        term_in.at[pl.ds(0, group - 1)], term_in.at[pl.ds(0, group - 1)], term_send, term_recv,
        device_id=peer(1), device_id_type=MESH,
    )
    all_term.wait()
    for b in range(n_sp):
        out[:, b * q_blk : (b + 1) * q_blk] = jnp.sum(term_in[pl.ds(b * n_tm, n_tm)], axis=0)

    all_rs.wait_send()
    all_ag.wait_send()
    for slot in range(1, n_sp):
        part_copy(slot, y).wait_send()
    halo(0).wait_send()
    halo(1).wait_send()


def solution(mesh):
    n_tm, n_sp = mesh.shape["tm"], mesh.shape["space"]

    def local(fm, q_frame, q_row, q_col, decay, taps, pw, out_w):
        frames, rows, width, ch = fm.shape
        n_q = q_frame.shape[0]
        n_pos = rows * width
        group = n_tm * n_sp
        per_home = n_q // group
        q_blk = n_q // n_sp
        half = n_q // 2
        dims = (n_tm, n_sp, n_q, rows, width, ch, rows * n_sp)
        smem = pl.BlockSpec(memory_space=pltpu.SMEM)
        vmem = pl.BlockSpec(memory_space=pltpu.VMEM)
        dma = pltpu.SemaphoreType.DMA
        out = pl.pallas_call(
            functools.partial(kernel, dims),
            out_shape=jax.ShapeDtypeStruct((2, n_q), F32),
            in_specs=[pl.BlockSpec(memory_space=pl.ANY), smem, smem, smem, vmem, vmem, vmem, vmem],
            out_specs=vmem,
            scratch_shapes=[
                pltpu.VMEM((n_pos, ch), BF16),
                pltpu.VMEM((n_pos + 8, ch), F32),
                pltpu.VMEM((ch + 16, n_pos), BF16),
                pltpu.VMEM((n_q, ch), F32),
                pltpu.VMEM((group, per_home, ch), BF16),
                pltpu.VMEM((group - 1, per_home, ch), BF16),
                pltpu.VMEM((per_home, ch), BF16),
                pltpu.VMEM((group, per_home, ch), BF16),
                pltpu.VMEM((ch, n_q), BF16),
                pltpu.VMEM((n_tm, 1, ch), F32),
                pltpu.VMEM((3, ch, q_blk), F32),
                pltpu.VMEM((ch, ch), BF16),
                pltpu.VMEM((n_tm, 2, ch), F32),
                pltpu.VMEM((n_pos, half), F32),
                pltpu.VMEM((ch + 16, half), F32),
                pltpu.VMEM((n_sp, ch + 16, q_blk), F32),
                pltpu.VMEM((n_sp - 1, ch + 16, q_blk), F32),
                pltpu.VMEM((ch, q_blk), BF16),
                pltpu.VMEM((2, ch, q_blk), BF16),
                pltpu.VMEM((n_tm, 2, q_blk), F32),
                pltpu.VMEM((group, 2, q_blk), F32),
                dma, dma, dma, dma, dma, dma, dma,
                dma((n_sp - 1,)), dma((n_sp - 1,)), dma((2,)), dma((2,)), dma, dma,
            ],
            compiler_params=pltpu.CompilerParams(collective_id=0, has_side_effects=True),
        )(fm.reshape(n_pos, ch), q_frame, q_row, q_col, decay, taps, pw, out_w)
        return out[None]

    placed = (
        P(("video", "tm"), "space", None, None),
        P("video"),
        P("video"),
        P("video"),
        P(("video", "tm"), None),
        P(),
        P(),
        P(),
    )
    return jax.shard_map(
        local, mesh=mesh, in_specs=placed, out_specs=P(("video", "tm"), None, None), check_vma=False
    )
```

```python
import functools
import math

import jax
import jax.numpy as jnp
from jax import lax
from jax.experimental import pallas as pl
from jax.experimental.pallas import tpu as pltpu
from jax.sharding import PartitionSpec as P

MESH = pl.DeviceIdType.MESH
F32 = jnp.float32
BF16 = jnp.bfloat16


def kernel(
    dims, fm, q_frame, q_row, q_col, decay, taps, pw, out_w, out,
    keys, keys32, keys_t, contrib32, contrib, rs_in, z_own, z_in, q_own, q_all, q_t, decay_all,
    tap_cols, pw_t, proj, even, odd, acc, part, part_in, att_own, att_in, term, term_in, row_own,
    row_all, key_sem, rs_send, rs_recv, z_send, z_recv, ag_send, ag_recv, dec_send, dec_recv,
    part_send, part_recv, halo_send, halo_recv, term_send, term_recv, row_send, row_recv,
):
    n_tm, n_sp, n_q, rows, width, ch, height = dims
    n_z = n_tm // 2
    plane = 2 * n_sp
    q_blk = n_q // n_sp
    n_pos = rows * width
    t = lax.axis_index("tm")
    y = lax.axis_index("space")
    z = lax.div(t, 2)
    core = lax.rem(t, 2)
    me = y * 2 + core

    def in_plane(r):
        other = lax.rem(me + r, plane)
        return other, {"tm": z * 2 + lax.rem(other, 2), "space": lax.div(other, 2)}

    def along_z(r):
        return {"tm": lax.rem(t + 2 * r, n_tm)}

    load = pltpu.make_async_copy(fm, keys, key_sem)
    load.start()
    barrier = pltpu.get_barrier_semaphore()
    for r in range(1, n_tm):
        pl.semaphore_signal(
            barrier, inc=1, device_id={"tm": lax.rem(t + r, n_tm)}, device_id_type=MESH
        )
    for r in range(1, n_sp):
        for c in range(2):
            pl.semaphore_signal(
                barrier, inc=1, device_id={"tm": z * 2 + c, "space": lax.rem(y + r, n_sp)},
                device_id_type=MESH,
            )
    load.wait()

    step = 256

    @pl.loop(0, n_pos // step)
    def _(j):
        at = pl.multiple_of(j * step, step)
        keys32[pl.ds(at, step), :] = keys[pl.ds(at, step), :].astype(F32)

    keys32[pl.ds(n_pos, 8), :] = jnp.zeros((8, ch), F32)
    first_row = y * rows

    @pl.loop(0, n_q // 8)
    def _(i):
        for u in range(8):
            q = i * 8 + u
            row = q_row[q] - first_row
            mine = (q_frame[q] == t) & (row >= 0) & (row < rows)
            at = jnp.where(mine, row * width + q_col[q], n_pos)
            contrib32[pl.ds(q, 1), :] = keys32[pl.ds(at, 1), :]

    contrib[...] = contrib32[...].reshape(plane, n_q // plane, ch).astype(BF16)

    pl.semaphore_wait(barrier, n_tm - 1 + plane - 2)

    def rs_copy(r):
        other, device = in_plane(r)
        return pltpu.make_async_remote_copy(
            contrib.at[other], rs_in.at[r - 1], rs_send, rs_recv,
            device_id=device, device_id_type=MESH,
        )

    for r in range(1, plane):
        rs_copy(r).start()

    decay_all[t] = decay[...]

    @pl.loop(1, n_tm)
    def _(r):
        pltpu.make_async_remote_copy(
            decay, decay_all.at[t], dec_send, dec_recv,
            device_id={"tm": lax.rem(t + r, n_tm)}, device_id_type=MESH,
        ).start()

    all_rs = pltpu.make_async_remote_copy(
        rs_in, rs_in, rs_send, rs_recv, device_id=in_plane(1)[1], device_id_type=MESH
    )
    all_rs.wait_recv()
    total = contrib[me].astype(F32) + jnp.sum(rs_in[...].astype(F32), axis=0)
    z_own[...] = total.astype(BF16)
    for r in range(1, n_z):
        pltpu.make_async_remote_copy(
            z_own, z_in.at[r - 1], z_send, z_recv, device_id=along_z(r), device_id_type=MESH
        ).start()

    @pl.loop(0, n_pos // 128)
    def _(j):
        at = pl.multiple_of(j * 128, 128)
        keys_t[pl.ds(0, ch), pl.ds(at, 128)] = keys32[pl.ds(at, 128), :].T.astype(BF16)

    place = lax.broadcasted_iota(jnp.int32, (16, n_pos), 1).astype(F32)
    line = jnp.floor((place + 0.5) * (1.0 / width))
    col = place - line * width
    line = line + (y * rows).astype(F32)
    kind = lax.broadcasted_iota(jnp.int32, (16, n_pos), 0)
    extra = jnp.where(kind == 0, 1.0, jnp.where(kind == 1, col, jnp.where(kind == 2, line, 0.0)))
    keys_t[pl.ds(ch, 16), :] = extra.astype(BF16)

    all_z = pltpu.make_async_remote_copy(
        z_in, z_in, z_send, z_recv, device_id=along_z(1), device_id_type=MESH
    )
    all_z.wait_recv()
    total = total + jnp.sum(z_in[...].astype(F32), axis=0)
    q_own[...] = total.astype(BF16)
    q_all[me] = total.astype(BF16)
    for r in range(1, plane):
        pltpu.make_async_remote_copy(
            q_own, q_all.at[me], ag_send, ag_recv, device_id=in_plane(r)[1], device_id_type=MESH
        ).start()

    eye = lax.broadcasted_iota(jnp.int32, (ch, ch), 0) == lax.broadcasted_iota(
        jnp.int32, (ch, ch), 1
    )
    for k in range(3):
        column = jnp.sum(jnp.where(eye, taps[pl.ds(k, 1), :], 0.0), axis=1, keepdims=True)
        tap_cols[k] = jnp.broadcast_to(column, (ch, q_blk))
    pw_t[...] = pw[...].astype(F32).T.astype(BF16)
    all_dec = pltpu.make_async_remote_copy(
        decay_all.at[pl.ds(0, n_tm - 1)], decay_all.at[pl.ds(0, n_tm - 1)], dec_send, dec_recv,
        device_id={"tm": lax.rem(t + 1, n_tm)}, device_id_type=MESH,
    )
    all_dec.wait()
    run = out_w[...] * (1.0 - decay[...])
    gain = jnp.zeros_like(run)
    for frame in range(n_tm):
        kept = gain if frame == 0 else gain * decay_all[frame]
        gain = jnp.where(t == frame, run, jnp.where(t < frame, kept, 0.0))
        proj[frame] = gain

    all_ag = pltpu.make_async_remote_copy(
        rs_in, rs_in, ag_send, ag_recv, device_id=in_plane(1)[1], device_id_type=MESH
    )
    all_ag.wait_recv()
    scaled = (q_all[...].astype(F32).reshape(n_q, ch) * (math.log2(math.e) / math.sqrt(ch))).T
    high = scaled.astype(BF16)
    q_t[pl.ds(0, ch), :] = high
    q_t[pl.ds(ch, ch), :] = (scaled - high.astype(F32)).astype(BF16)

    half = n_q // 2
    pair = lax.div(y, 2)
    tile = 768
    n_tiles = n_pos // tile

    def part_copy(slot, to):
        return pltpu.make_async_remote_copy(
            part.at[slot], part_in.at[slot - 1], part_send.at[slot - 1], part_recv.at[slot - 1],
            device_id={"space": to}, device_id_type=MESH,
        )

    def score(buf, j, q_at):
        k = keys[pl.ds(pl.multiple_of(j * tile, tile), tile), :]
        s = jnp.dot(
            jnp.concatenate([k, k], axis=1), q_t[:, pl.ds(q_at, half)],
            preferred_element_type=F32,
        )
        buf[...] = s
        return jnp.max(jnp.max(s.reshape(tile // 8, 8, half), axis=0), axis=0, keepdims=True)

    def gather(buf, j, top, fade):
        e = jnp.exp2(buf[...] - top).astype(BF16)
        at = pl.multiple_of(j * tile, tile)
        acc[...] = acc[...] * fade + jnp.dot(
            keys_t[:, pl.ds(at, tile)], e, preferred_element_type=F32
        )

    def raised(top, seen):
        higher = jnp.maximum(top, seen)
        return higher, jnp.exp2(top - higher)

    q_ats = [
        pl.multiple_of((1 - pair) * half, half), pl.multiple_of(pair * half, half)
    ]
    top = score(even, 0, q_ats[0])
    for chunk in range(2):
        which = (1 - pair) if chunk == 0 else pair
        q_at = q_ats[chunk]
        acc[...] = jnp.zeros_like(acc)

        def two(i, carry):
            top, fade = carry
            seen = score(odd, 2 * i + 1, q_at)
            gather(even, 2 * i, top, fade)
            top, fade = raised(top, seen)
            seen = score(even, 2 * i + 2, q_at)
            gather(odd, 2 * i + 1, top, fade)
            return raised(top, seen)

        top, fade = lax.fori_loop(
            0, n_tiles // 2 - 1, two, (top, jnp.ones((1, half), F32))
        )
        seen = score(odd, n_tiles - 1, q_at)
        gather(even, n_tiles - 2, top, fade)
        top, fade = raised(top, seen)
        if chunk == 0:
            next_top = score(even, 0, q_ats[1])
        gather(odd, n_tiles - 1, top, fade)

        for side in range(2):
            to = which * 2 + side
            slot = lax.rem(to - y + n_sp, n_sp)
            lanes = slice(side * q_blk, (side + 1) * q_blk)
            part[slot, pl.ds(0, ch + 8), :] = acc[pl.ds(0, ch + 8), lanes]
            part[slot, pl.ds(ch + 8, 8), :] = jnp.broadcast_to(top[:, lanes], (8, q_blk))
            if chunk == 0:
                part_copy(slot, to).start()
            else:

                @pl.when(slot != 0)
                def _():
                    part_copy(slot, to).start()

        if chunk == 0:
            top = next_top

    for slot in range(1, n_sp):
        part_copy(slot, y).wait_recv()
    own = part[0]
    parts = [own] + [part_in[i] for i in range(n_sp - 1)]
    tops = [p[ch + 8 : ch + 9] for p in parts]
    best = functools.reduce(jnp.maximum, tops)
    mixed = None
    for p, m in zip(parts, tops):
        v = p[: ch + 8] * jnp.exp2(m - best)
        mixed = v if mixed is None else mixed + v
    inverse = 1.0 / mixed[ch : ch + 1]
    position = mixed[ch + 1 : ch + 3] * inverse
    unit = jnp.where(
        lax.broadcasted_iota(jnp.int32, (2, q_blk), 0) == 0, 1.0 / width, 1.0 / height
    )
    position = position * unit
    att = (mixed[:ch] * inverse).astype(BF16)
    att_own[...] = att

    def halo(side):
        to = lax.rem(t + (1 if side == 0 else n_tm - 1), n_tm)
        return pltpu.make_async_remote_copy(
            att_own, att_in.at[side], halo_send.at[side], halo_recv.at[side],
            device_id={"tm": to}, device_id_type=MESH,
        )

    halo(0).start()
    halo(1).start()
    att = att.astype(F32)
    mid = att * tap_cols[1]
    halo(0).wait_recv()
    halo(1).wait_recv()
    before = jnp.where(t > 0, att_in[0].astype(F32), 0.0)
    after = jnp.where(t < n_tm - 1, att_in[1].astype(F32), 0.0)
    depth = tap_cols[0] * before + mid + tap_cols[2] * after
    hidden = jax.nn.gelu(depth).astype(BF16)
    refined = att + jnp.dot(pw_t[...], hidden, preferred_element_type=F32)
    terms = jnp.dot(
        proj[...].reshape(2 * n_tm, ch), refined, preferred_element_type=F32,
        precision=lax.Precision.HIGHEST,
    )
    term[...] = terms.reshape(n_tm, 2, q_blk)

    def term_copy(source, target, slot):
        return pltpu.make_async_remote_copy(
            term.at[target], term_in.at[source], term_send.at[slot], term_recv.at[source],
            device_id={"tm": target}, device_id_type=MESH,
        )

    for r in range(1, n_tm):

        @pl.when(t + r < n_tm)
        def _():
            term_copy(t, t + r, r).start()

    for source in range(n_tm - 1):

        @pl.when(source < t)
        def _():
            term_copy(source, t, 0).wait_recv()

    track = term[t] + position
    for source in range(n_tm - 1):
        track = track + jnp.where(source < t, term_in[source], 0.0)
    row_own[...] = track
    row_all[y] = track
    for r in range(1, n_sp):
        pltpu.make_async_remote_copy(
            row_own, row_all.at[y], row_send, row_recv,
            device_id={"space": lax.rem(y + r, n_sp)}, device_id_type=MESH,
        ).start()
    all_row = pltpu.make_async_remote_copy(
        row_all.at[pl.ds(0, n_sp - 1)], row_all.at[pl.ds(0, n_sp - 1)], row_send, row_recv,
        device_id={"space": lax.rem(y + 1, n_sp)}, device_id_type=MESH,
    )
    all_row.wait()
    for b in range(n_sp):
        out[:, b * q_blk : (b + 1) * q_blk] = row_all[b]

    all_rs.wait_send()
    all_z.wait_send()
    all_ag.wait_send()
    for slot in range(1, n_sp):
        part_copy(slot, y).wait_send()
    halo(0).wait_send()
    halo(1).wait_send()
    for r in range(1, n_tm):

        @pl.when(t + r < n_tm)
        def _():
            term_copy(t, t + r, r).wait_send()


def solution(mesh):
    n_tm, n_sp = mesh.shape["tm"], mesh.shape["space"]

    def local(fm, q_frame, q_row, q_col, decay, taps, pw, out_w):
        frames, rows, width, ch = fm.shape
        n_q = q_frame.shape[0]
        n_pos = rows * width
        plane = 2 * n_sp
        n_z = n_tm // 2
        home = n_q // plane
        q_blk = n_q // n_sp
        half = n_q // 2
        dims = (n_tm, n_sp, n_q, rows, width, ch, rows * n_sp)
        smem = pl.BlockSpec(memory_space=pltpu.SMEM)
        vmem = pl.BlockSpec(memory_space=pltpu.VMEM)
        dma = pltpu.SemaphoreType.DMA
        out = pl.pallas_call(
            functools.partial(kernel, dims),
            out_shape=jax.ShapeDtypeStruct((2, n_q), F32),
            in_specs=[pl.BlockSpec(memory_space=pl.ANY), smem, smem, smem, vmem, vmem, vmem, vmem],
            out_specs=vmem,
            scratch_shapes=[
                pltpu.VMEM((n_pos, ch), BF16),
                pltpu.VMEM((n_pos + 8, ch), F32),
                pltpu.VMEM((ch + 16, n_pos), BF16),
                pltpu.VMEM((n_q, ch), F32),
                pltpu.VMEM((plane, home, ch), BF16),
                pltpu.VMEM((plane - 1, home, ch), BF16),
                pltpu.VMEM((home, ch), BF16),
                pltpu.VMEM((n_z - 1, home, ch), BF16),
                pltpu.VMEM((home, ch), BF16),
                pltpu.VMEM((plane, home, ch), BF16),
                pltpu.VMEM((2 * ch, n_q), BF16),
                pltpu.VMEM((n_tm, 1, ch), F32),
                pltpu.VMEM((3, ch, q_blk), F32),
                pltpu.VMEM((ch, ch), BF16),
                pltpu.VMEM((n_tm, 2, ch), F32),
                pltpu.VMEM((768, half), F32),
                pltpu.VMEM((768, half), F32),
                pltpu.VMEM((ch + 16, half), F32),
                pltpu.VMEM((n_sp, ch + 16, q_blk), F32),
                pltpu.VMEM((n_sp - 1, ch + 16, q_blk), F32),
                pltpu.VMEM((ch, q_blk), BF16),
                pltpu.VMEM((2, ch, q_blk), BF16),
                pltpu.VMEM((n_tm, 2, q_blk), F32),
                pltpu.VMEM((n_tm - 1, 2, q_blk), F32),
                pltpu.VMEM((2, q_blk), F32),
                pltpu.VMEM((n_sp, 2, q_blk), F32),
                dma, dma, dma, dma, dma, dma, dma, dma, dma,
                dma((n_sp - 1,)), dma((n_sp - 1,)), dma((2,)), dma((2,)),
                dma((n_tm,)), dma((n_tm - 1,)), dma, dma,
            ],
            compiler_params=pltpu.CompilerParams(collective_id=0, has_side_effects=True),
        )(fm.reshape(n_pos, ch), q_frame, q_row, q_col, decay, taps, pw, out_w)
        return out[None]

    placed = (
        P(("video", "tm"), "space", None, None),
        P("video"),
        P("video"),
        P("video"),
        P(("video", "tm"), None),
        P(),
        P(),
        P(),
    )
    return jax.shard_map(
        local, mesh=mesh, in_specs=placed, out_specs=P(("video", "tm"), None, None), check_vma=False
    )
```

```python
import functools
import math

import jax
import jax.numpy as jnp
from jax import lax
from jax.experimental import pallas as pl
from jax.experimental.pallas import tpu as pltpu
from jax.sharding import PartitionSpec as P

MESH = pl.DeviceIdType.MESH
F32 = jnp.float32
BF16 = jnp.bfloat16


def far_first(n):
    return sorted(range(1, n), key=lambda r: -min(r, n - r))


def kernel(
    dims, fm, q_frame, q_row, q_col, decay, taps, pw, out_w, out,
    rows_v, rows_s, keys, keys32, keys_t, contrib32, contrib, rs_in, z_own, z_in, q_own, q_all, q_t, decay_all,
    tap_cols, pw_t, proj, even, odd, acc, part, part_in, att_own, att_in, term, term_in,
    key_sem, row_sem, rs_send, rs_recv, z_send, z_recv, ag_send, ag_recv, dec_send, dec_recv,
    part_send, part_recv, halo_send, halo_recv, term_send, term_recv,
):
    n_tm, n_sp, n_q, rows, width, ch, height = dims
    n_z = n_tm // 2
    plane = 2 * n_sp
    q_blk = n_q // n_sp
    n_pos = rows * width
    t = lax.axis_index("tm")
    y = lax.axis_index("space")
    z = lax.div(t, 2)
    core = lax.rem(t, 2)
    me = y * 2 + core

    def in_plane(r):
        other = lax.rem(me + r, plane)
        return other, {"tm": z * 2 + lax.rem(other, 2), "space": lax.div(other, 2)}

    def along_z(r):
        return {"tm": lax.rem(t + 2 * r, n_tm)}

    n_loads = 4
    piece = n_pos // n_loads

    def load(i):
        cut = pl.ds(i * piece, piece)
        return pltpu.make_async_copy(fm.at[cut], keys.at[cut], key_sem.at[i])

    for i in range(n_loads):
        load(i).start()
    line = q_frame[...] * height + q_row[...] - (t * height + y * rows)
    mine = (line >= 0) & (line < rows)
    rows_v[...] = jnp.where(mine, line * width + q_col[...], n_pos)
    tell = pltpu.make_async_copy(rows_v, rows_s, row_sem)
    tell.start()
    barrier = pltpu.get_barrier_semaphore()
    for r in range(1, n_tm):
        pl.semaphore_signal(
            barrier, inc=1, device_id={"tm": lax.rem(t + r, n_tm)}, device_id_type=MESH
        )
    for r in range(1, n_sp):
        for c in range(2):
            pl.semaphore_signal(
                barrier, inc=1, device_id={"tm": z * 2 + c, "space": lax.rem(y + r, n_sp)},
                device_id_type=MESH,
            )
    step = 384
    keys32[pl.ds(n_pos, 8), :] = jnp.zeros((8, ch), F32)
    for i in range(n_loads):
        load(i).wait()

        @pl.loop(0, piece // step)
        def _(j):
            at = pl.multiple_of(i * piece + j * step, step)
            keys32[pl.ds(at, step), :] = keys[pl.ds(at, step), :].astype(F32)

    tell.wait()
    for b in range(n_q // 128):

        @pl.loop(0, 8)
        def _(i):
            for u in range(16):
                at = rows_s[b, i * 16 + u]
                contrib32[pl.ds(b * 128 + i * 16 + u, 1), :] = keys32[pl.ds(at, 1), :]

    contrib[...] = contrib32[...].reshape(plane, n_q // plane, ch).astype(BF16)

    pl.semaphore_wait(barrier, n_tm - 1 + plane - 2)

    def rs_copy(r):
        other, device = in_plane(r)
        return pltpu.make_async_remote_copy(
            contrib.at[other], rs_in.at[r - 1], rs_send, rs_recv,
            device_id=device, device_id_type=MESH,
        )

    for r in far_first(plane):
        rs_copy(r).start()

    decay_all[t] = decay[...]

    @pl.loop(1, n_tm)
    def _(r):
        pltpu.make_async_remote_copy(
            decay, decay_all.at[t], dec_send, dec_recv,
            device_id={"tm": lax.rem(t + r, n_tm)}, device_id_type=MESH,
        ).start()

    all_rs = pltpu.make_async_remote_copy(
        rs_in, rs_in, rs_send, rs_recv, device_id=in_plane(1)[1], device_id_type=MESH
    )
    all_rs.wait_recv()
    total = contrib[me].astype(F32) + jnp.sum(rs_in[...].astype(F32), axis=0)
    z_own[...] = total.astype(BF16)
    for r in far_first(n_z):
        pltpu.make_async_remote_copy(
            z_own, z_in.at[r - 1], z_send, z_recv, device_id=along_z(r), device_id_type=MESH
        ).start()

    @pl.loop(0, n_pos // 128)
    def _(j):
        at = pl.multiple_of(j * 128, 128)
        keys_t[pl.ds(0, ch), pl.ds(at, 128)] = keys32[pl.ds(at, 128), :].T.astype(BF16)

    place = lax.broadcasted_iota(jnp.int32, (16, n_pos), 1).astype(F32)
    line = jnp.floor((place + 0.5) * (1.0 / width))
    col = place - line * width
    line = line + (y * rows).astype(F32)
    kind = lax.broadcasted_iota(jnp.int32, (16, n_pos), 0)
    extra = jnp.where(kind == 0, 1.0, jnp.where(kind == 1, col, jnp.where(kind == 2, line, 0.0)))
    keys_t[pl.ds(ch, 16), :] = extra.astype(BF16)

    all_z = pltpu.make_async_remote_copy(
        z_in, z_in, z_send, z_recv, device_id=along_z(1), device_id_type=MESH
    )
    all_z.wait_recv()
    total = total + jnp.sum(z_in[...].astype(F32), axis=0)
    q_own[...] = total.astype(BF16)
    q_all[me] = total.astype(BF16)
    for r in far_first(plane):
        pltpu.make_async_remote_copy(
            q_own, q_all.at[me], ag_send, ag_recv, device_id=in_plane(r)[1], device_id_type=MESH
        ).start()

    eye = lax.broadcasted_iota(jnp.int32, (ch, ch), 0) == lax.broadcasted_iota(
        jnp.int32, (ch, ch), 1
    )
    for k in range(3):
        column = jnp.sum(jnp.where(eye, taps[pl.ds(k, 1), :], 0.0), axis=1, keepdims=True)
        tap_cols[k] = jnp.broadcast_to(column, (ch, q_blk))
    pw_t[...] = pw[...].astype(F32).T.astype(BF16)
    all_dec = pltpu.make_async_remote_copy(
        decay_all.at[pl.ds(0, n_tm - 1)], decay_all.at[pl.ds(0, n_tm - 1)], dec_send, dec_recv,
        device_id={"tm": lax.rem(t + 1, n_tm)}, device_id_type=MESH,
    )
    all_dec.wait()
    run = out_w[...] * (1.0 - decay[...])
    gain = jnp.zeros_like(run)
    for frame in range(n_tm):
        kept = gain if frame == 0 else gain * decay_all[frame]
        gain = jnp.where(t == frame, run, jnp.where(t < frame, kept, 0.0))
        proj[frame] = gain

    all_ag = pltpu.make_async_remote_copy(
        rs_in, rs_in, ag_send, ag_recv, device_id=in_plane(1)[1], device_id_type=MESH
    )
    all_ag.wait_recv()
    q_t[...] = q_all[...].astype(F32).reshape(n_q, ch).T.astype(BF16)

    half = n_q // 2
    pair = lax.div(y, 2)
    scale = math.log2(math.e) / math.sqrt(ch)

    def part_copy(slot, to):
        return pltpu.make_async_remote_copy(
            part.at[slot], part_in.at[slot - 1], part_send.at[slot - 1], part_recv.at[slot - 1],
            device_id={"space": to}, device_id_type=MESH,
        )

    def score(buf, at, size, q_at):
        s = jnp.dot(
            keys[pl.ds(at, size), :], q_t[:, pl.ds(q_at, half)], preferred_element_type=F32
        )
        buf[pl.ds(at, size), :] = s
        return jnp.max(s.reshape(size // 8, 8, half), axis=0)

    def weigh(buf, at, size, top):
        e = jnp.exp2((buf[pl.ds(at, size), :] - top) * scale).astype(BF16)
        acc[...] += jnp.dot(keys_t[:, pl.ds(at, size)], e, preferred_element_type=F32)

    def hand_over(which, top, last):
        for side in range(2):
            to = which * 2 + side
            slot = lax.rem(to - y + n_sp, n_sp)
            lanes = slice(side * q_blk, (side + 1) * q_blk)
            part[slot, pl.ds(0, ch + 8), :] = acc[pl.ds(0, ch + 8), lanes]
            part[slot, pl.ds(ch + 8, 8), :] = jnp.broadcast_to(top[:, lanes], (8, q_blk))
            if last:

                @pl.when(slot != 0)
                def _():
                    part_copy(slot, to).start()
            else:
                part_copy(slot, to).start()

    far, near = 1 - pair, pair
    step_both, step_last = n_pos // 3, n_pos // 2
    top_far = score(even, 0, n_pos, pl.multiple_of(far * half, half))
    top_far = jnp.max(top_far, axis=0, keepdims=True)
    acc[...] = jnp.zeros_like(acc)

    def both(j, top):
        at = pl.multiple_of(j * step_both, step_both)
        top = jnp.maximum(top, score(odd, at, step_both, pl.multiple_of(near * half, half)))
        weigh(even, at, step_both, top_far)
        return top

    top_near = lax.fori_loop(0, 3, both, jnp.full((8, half), -jnp.inf, F32))
    top_near = jnp.max(top_near, axis=0, keepdims=True)
    hand_over(far, top_far, False)
    acc[...] = jnp.zeros_like(acc)

    @pl.loop(0, 2)
    def _(j):
        weigh(odd, pl.multiple_of(j * step_last, step_last), step_last, top_near)

    hand_over(near, top_near, True)

    for slot in range(1, n_sp):
        part_copy(slot, y).wait_recv()
    own = part[0]
    parts = [own] + [part_in[i] for i in range(n_sp - 1)]
    tops = [p[ch + 8 : ch + 9] for p in parts]
    best = functools.reduce(jnp.maximum, tops)
    mixed = None
    for p, m in zip(parts, tops):
        v = p[: ch + 8] * jnp.exp2((m - best) * scale)
        mixed = v if mixed is None else mixed + v
    inverse = 1.0 / mixed[ch : ch + 1]
    position = mixed[ch + 1 : ch + 3] * inverse
    unit = jnp.where(
        lax.broadcasted_iota(jnp.int32, (2, q_blk), 0) == 0, 1.0 / width, 1.0 / height
    )
    position = position * unit
    att = (mixed[:ch] * inverse).astype(BF16)
    att_own[...] = att

    def halo(side):
        to = lax.rem(t + (1 if side == 0 else n_tm - 1), n_tm)
        return pltpu.make_async_remote_copy(
            att_own, att_in.at[side], halo_send.at[side], halo_recv.at[side],
            device_id={"tm": to}, device_id_type=MESH,
        )

    halo(0).start()
    halo(1).start()
    att = att.astype(F32)
    mid = att * tap_cols[1]
    halo(0).wait_recv()
    halo(1).wait_recv()
    before = jnp.where(t > 0, att_in[0].astype(F32), 0.0)
    after = jnp.where(t < n_tm - 1, att_in[1].astype(F32), 0.0)
    depth = tap_cols[0] * before + mid + tap_cols[2] * after
    hidden = jax.nn.gelu(depth).astype(BF16)
    refined = att + jnp.dot(pw_t[...], hidden, preferred_element_type=F32)
    terms = jnp.dot(
        proj[...].reshape(2 * n_tm, ch), refined, preferred_element_type=F32,
        precision=lax.Precision.HIGHEST,
    )
    term[...] = terms.reshape(n_tm, 2, q_blk)

    own = term[t] + position
    term[t] = own
    term_in[t, y] = own

    def term_copy(r, k):
        return pltpu.make_async_remote_copy(
            term.at[t + r], term_in.at[t, y], term_send.at[r], term_recv.at[t],
            device_id={"tm": t + r, "space": lax.rem(y + k, n_sp)}, device_id_type=MESH,
        )

    def terms_of(source, count, slot):
        some = term_in.at[source, pl.ds(0, count)]
        return pltpu.make_async_remote_copy(
            some, some, term_send.at[slot], term_recv.at[source],
            device_id={"space": lax.rem(y + 1, n_sp)}, device_id_type=MESH,
        )

    for k in range(1, n_sp):
        term_copy(0, k).start()
    for r in range(1, n_tm):

        @pl.when(t + r < n_tm)
        def _():
            for k in range(n_sp):
                term_copy(r, k).start()

    for source in range(n_tm - 1):

        @pl.when(source < t)
        def _():
            terms_of(source, n_sp, 0).wait_recv()

    terms_of(t, n_sp - 1, 0).wait()
    for b in range(n_sp):
        track = term_in[t, b]
        for source in range(n_tm - 1):
            track = track + jnp.where(source < t, term_in[source, b], 0.0)
        out[:, b * q_blk : (b + 1) * q_blk] = track

    all_rs.wait_send()
    all_z.wait_send()
    all_ag.wait_send()
    for slot in range(1, n_sp):
        part_copy(slot, y).wait_send()
    halo(0).wait_send()
    halo(1).wait_send()
    for r in range(1, n_tm):

        @pl.when(t + r < n_tm)
        def _():
            terms_of(0, n_sp, r).wait_send()


def solution(mesh):
    n_tm, n_sp = mesh.shape["tm"], mesh.shape["space"]

    def local(fm, q_frame, q_row, q_col, decay, taps, pw, out_w):
        frames, rows, width, ch = fm.shape
        n_q = q_frame.shape[0]
        n_pos = rows * width
        plane = 2 * n_sp
        n_z = n_tm // 2
        home = n_q // plane
        q_blk = n_q // n_sp
        half = n_q // 2
        dims = (n_tm, n_sp, n_q, rows, width, ch, rows * n_sp)
        vmem = pl.BlockSpec(memory_space=pltpu.VMEM)
        dma = pltpu.SemaphoreType.DMA
        queries = [a.reshape(n_q // 128, 128) for a in (q_frame, q_row, q_col)]
        out = pl.pallas_call(
            functools.partial(kernel, dims),
            out_shape=jax.ShapeDtypeStruct((2, n_q), F32),
            in_specs=[pl.BlockSpec(memory_space=pl.ANY)] + [vmem] * 7,
            out_specs=vmem,
            scratch_shapes=[
                pltpu.VMEM((n_q // 128, 128), jnp.int32),
                pltpu.SMEM((n_q // 128, 128), jnp.int32),
                pltpu.VMEM((n_pos, ch), BF16),
                pltpu.VMEM((n_pos + 8, ch), F32),
                pltpu.VMEM((ch + 16, n_pos), BF16),
                pltpu.VMEM((n_q, ch), F32),
                pltpu.VMEM((plane, home, ch), BF16),
                pltpu.VMEM((plane - 1, home, ch), BF16),
                pltpu.VMEM((home, ch), BF16),
                pltpu.VMEM((n_z - 1, home, ch), BF16),
                pltpu.VMEM((home, ch), BF16),
                pltpu.VMEM((plane, home, ch), BF16),
                pltpu.VMEM((ch, n_q), BF16),
                pltpu.VMEM((n_tm, 1, ch), F32),
                pltpu.VMEM((3, ch, q_blk), F32),
                pltpu.VMEM((ch, ch), BF16),
                pltpu.VMEM((n_tm, 2, ch), F32),
                pltpu.VMEM((n_pos, half), F32),
                pltpu.VMEM((n_pos, half), F32),
                pltpu.VMEM((ch + 16, half), F32),
                pltpu.VMEM((n_sp, ch + 16, q_blk), F32),
                pltpu.VMEM((n_sp - 1, ch + 16, q_blk), F32),
                pltpu.VMEM((ch, q_blk), BF16),
                pltpu.VMEM((2, ch, q_blk), BF16),
                pltpu.VMEM((n_tm, 2, q_blk), F32),
                pltpu.VMEM((n_tm, n_sp, 2, q_blk), F32),
                dma((4,)), dma, dma, dma, dma, dma, dma, dma, dma, dma,
                dma((n_sp - 1,)), dma((n_sp - 1,)), dma((2,)), dma((2,)),
                dma((n_tm,)), dma((n_tm,)),
            ],
            compiler_params=pltpu.CompilerParams(collective_id=0, has_side_effects=True),
        )(fm.reshape(n_pos, ch), *queries, decay, taps, pw, out_w)
        return out[None]

    placed = (
        P(("video", "tm"), "space", None, None),
        P("video"),
        P("video"),
        P("video"),
        P(("video", "tm"), None),
        P(),
        P(),
        P(),
    )
    return jax.shard_map(
        local, mesh=mesh, in_specs=placed, out_specs=P(("video", "tm"), None, None), check_vma=False
    )
```

```python
import functools
import math

import jax
import jax.numpy as jnp
from jax import lax
from jax.experimental import pallas as pl
from jax.experimental.pallas import tpu as pltpu
from jax.sharding import PartitionSpec as P

MESH = pl.DeviceIdType.MESH
F32 = jnp.float32
BF16 = jnp.bfloat16
SIB = jnp.bfloat16


def far_first(n):
    return sorted(range(1, n), key=lambda r: -min(r, n - r))


def kernel(
    dims, fm, q_frame, q_row, q_col, decay, taps, pw, out_w, out,
    rows_v, rows_s, keys, keys32, keys_t, contrib32, contrib, rs_in, z_own, z_in, q_own, q_all, q_far, q_near, decay_all,
    tap_cols, pw_t, proj, even, odd, acc_far, acc, part, part_in, sib_out, sib_in, sib_facts,
    sib_facts_in, att_own, att_in, term, term_in,
    key_sem, row_sem, rs_send, rs_recv, z_send, z_recv, ag_send, ag_recv, on_send,
    on_recv, dec_send, dec_recv,
    part_send, part_recv, sib_send, sib_recv, halo_send, halo_recv, term_send, term_recv,
):
    n_tm, n_sp, n_q, rows, width, ch, height = dims
    n_z = n_tm // 2
    plane = 2 * n_sp
    q_blk = n_q // n_sp
    n_pos = rows * width
    t = lax.axis_index("tm")
    y = lax.axis_index("space")
    z = lax.div(t, 2)
    core = lax.rem(t, 2)
    me = y * 2 + core

    def in_plane(r):
        other = lax.rem(me + r, plane)
        return other, {"tm": z * 2 + lax.rem(other, 2), "space": lax.div(other, 2)}

    def along_z(r):
        return {"tm": lax.rem(t + 2 * r, n_tm)}

    n_loads = 4
    piece = n_pos // n_loads

    def load(i):
        cut = pl.ds(i * piece, piece)
        return pltpu.make_async_copy(fm.at[cut], keys.at[cut], key_sem.at[i])

    for i in range(n_loads):
        load(i).start()
    line = q_frame[...] * height + q_row[...] - (t * height + y * rows)
    mine = (line >= 0) & (line < rows)
    rows_v[...] = jnp.where(mine, line * width + q_col[...], n_pos)
    tell = pltpu.make_async_copy(rows_v, rows_s, row_sem)
    tell.start()
    barrier = pltpu.get_barrier_semaphore()
    for r in range(1, n_tm):
        pl.semaphore_signal(
            barrier, inc=1, device_id={"tm": lax.rem(t + r, n_tm)}, device_id_type=MESH
        )
    for r in range(1, n_sp):
        for c in range(2):
            pl.semaphore_signal(
                barrier, inc=1, device_id={"tm": z * 2 + c, "space": lax.rem(y + r, n_sp)},
                device_id_type=MESH,
            )
    step = 384
    keys32[pl.ds(n_pos, 8), :] = jnp.zeros((8, ch), F32)
    for i in range(n_loads):
        load(i).wait()

        @pl.loop(0, piece // step)
        def _(j):
            at = pl.multiple_of(i * piece + j * step, step)
            keys32[pl.ds(at, step), :] = keys[pl.ds(at, step), :].astype(F32)

    tell.wait()
    for b in range(n_q // 128):

        @pl.loop(0, 8)
        def _(i):
            for u in range(16):
                at = rows_s[b, i * 16 + u]
                contrib32[pl.ds(b * 128 + i * 16 + u, 1), :] = keys32[pl.ds(at, 1), :]

    contrib[...] = contrib32[...].reshape(plane, n_q // plane, ch).astype(BF16)

    pl.semaphore_wait(barrier, n_tm - 1 + plane - 2)

    def rs_copy(r):
        other, device = in_plane(r)
        return pltpu.make_async_remote_copy(
            contrib.at[other], rs_in.at[r - 1], rs_send, rs_recv,
            device_id=device, device_id_type=MESH,
        )

    for r in far_first(plane):
        rs_copy(r).start()

    decay_all[t] = decay[...]

    @pl.loop(1, n_tm)
    def _(r):
        pltpu.make_async_remote_copy(
            decay, decay_all.at[t], dec_send, dec_recv,
            device_id={"tm": lax.rem(t + r, n_tm)}, device_id_type=MESH,
        ).start()

    all_rs = pltpu.make_async_remote_copy(
        rs_in, rs_in, rs_send, rs_recv, device_id=in_plane(1)[1], device_id_type=MESH
    )
    all_rs.wait_recv()
    total = contrib[me].astype(F32) + jnp.sum(rs_in[...].astype(F32), axis=0)
    z_own[...] = total.astype(BF16)
    for r in far_first(n_z):
        pltpu.make_async_remote_copy(
            z_own, z_in.at[r - 1], z_send, z_recv, device_id=along_z(r), device_id_type=MESH
        ).start()

    @pl.loop(0, n_pos // 128)
    def _(j):
        at = pl.multiple_of(j * 128, 128)
        keys_t[pl.ds(0, ch), pl.ds(at, 128)] = keys32[pl.ds(at, 128), :].T.astype(BF16)

    place = lax.broadcasted_iota(jnp.int32, (16, n_pos), 1).astype(F32)
    line = jnp.floor((place + 0.5) * (1.0 / width))
    col = place - line * width
    line = line + (y * rows).astype(F32)
    kind = lax.broadcasted_iota(jnp.int32, (16, n_pos), 0)
    extra = jnp.where(kind == 0, 1.0, jnp.where(kind == 1, col, jnp.where(kind == 2, line, 0.0)))
    keys_t[pl.ds(ch, 16), :] = extra.astype(BF16)

    all_z = pltpu.make_async_remote_copy(
        z_in, z_in, z_send, z_recv, device_id=along_z(1), device_id_type=MESH
    )
    all_z.wait_recv()
    total = total + jnp.sum(z_in[...].astype(F32), axis=0)
    q_own[...] = total.astype(BF16)
    q_all[me] = total.astype(BF16)
    on_chip = pltpu.make_async_remote_copy(
        q_own, q_all.at[me], on_send, on_recv, device_id={"tm": t + 1 - 2 * core},
        device_id_type=MESH,
    )
    on_chip.start()
    for k in far_first(n_sp):
        for c in range(2):
            pltpu.make_async_remote_copy(
                q_own, q_all.at[me], ag_send, ag_recv,
                device_id={"tm": z * 2 + c, "space": lax.rem(y + k, n_sp)}, device_id_type=MESH,
            ).start()

    pair = lax.div(y, 2)
    scale = math.log2(math.e) / math.sqrt(ch)

    def turned(first, count):
        return q_all[pl.ds(first, count)].astype(F32).reshape(-1, ch).T.astype(BF16)

    def score(buf, q, at, size):
        s = jnp.dot(keys[pl.ds(at, size), :], q[...], preferred_element_type=F32)
        buf[pl.ds(at, size), :] = s
        return jnp.max(s.reshape(size // 8, 8, s.shape[1]), axis=0)

    def weigh(buf, total, at, size, top):
        e = jnp.exp2((buf[pl.ds(at, size), :] - top) * scale).astype(BF16)
        total[...] += jnp.dot(keys_t[:, pl.ds(at, size)], e, preferred_element_type=F32)

    step_both, step_last = n_pos // 3, n_pos // 2

    on_chip.wait_recv()
    q_near[...] = turned(2 * y, 2)
    top_own = jnp.max(score(odd, q_near, 0, n_pos), axis=0, keepdims=True)
    acc[...] = jnp.zeros_like(acc)

    @pl.loop(0, 2)
    def _(j):
        weigh(odd, acc, pl.multiple_of(j * step_last, step_last), step_last, top_own)

    part[2, pl.ds(0, ch + 8), :] = acc[pl.ds(0, ch + 8), :]
    part[2, pl.ds(ch + 8, 8), :] = jnp.broadcast_to(top_own, (8, q_blk))

    eye = lax.broadcasted_iota(jnp.int32, (ch, ch), 0) == lax.broadcasted_iota(
        jnp.int32, (ch, ch), 1
    )
    for k in range(3):
        column = jnp.sum(jnp.where(eye, taps[pl.ds(k, 1), :], 0.0), axis=1, keepdims=True)
        tap_cols[k] = jnp.broadcast_to(column, (ch, q_blk))
    pw_t[...] = pw[...].astype(F32).T.astype(BF16)
    all_dec = pltpu.make_async_remote_copy(
        decay_all.at[pl.ds(0, n_tm - 1)], decay_all.at[pl.ds(0, n_tm - 1)], dec_send, dec_recv,
        device_id={"tm": lax.rem(t + 1, n_tm)}, device_id_type=MESH,
    )
    all_dec.wait()
    run = out_w[...] * (1.0 - decay[...])
    gain = jnp.zeros_like(run)
    for frame in range(n_tm):
        kept = gain if frame == 0 else gain * decay_all[frame]
        gain = jnp.where(t == frame, run, jnp.where(t < frame, kept, 0.0))
        proj[frame] = gain

    all_ag = pltpu.make_async_remote_copy(
        q_all.at[pl.ds(0, plane - 2)], q_all.at[pl.ds(0, plane - 2)], ag_send, ag_recv,
        device_id=in_plane(1)[1], device_id_type=MESH,
    )
    all_ag.wait_recv()
    far = 1 - pair
    sib = y + 1 - 2 * lax.rem(y, 2)
    q_far[...] = turned(4 * far, 4)
    q_near[...] = turned(2 * sib, 2)
    top_far = jnp.max(score(even, q_far, 0, n_pos), axis=0, keepdims=True)
    acc_far[...] = jnp.zeros_like(acc_far)

    def both(j, top):
        at = pl.multiple_of(j * step_both, step_both)
        top = jnp.maximum(top, score(odd, q_near, at, step_both))
        weigh(even, acc_far, at, step_both, top_far)
        return top

    top_sib = lax.fori_loop(0, 3, both, jnp.full((8, q_blk), -jnp.inf, F32))
    top_sib = jnp.max(top_sib, axis=0, keepdims=True)

    def part_copy(side):
        return pltpu.make_async_remote_copy(
            part.at[side], part_in.at[lax.rem(y, 2)], part_send.at[side],
            part_recv.at[lax.rem(y, 2)], device_id={"space": far * 2 + side}, device_id_type=MESH,
        )

    def part_arrival(side):
        return pltpu.make_async_remote_copy(
            part.at[side], part_in.at[side], part_send.at[side], part_recv.at[side],
            device_id={"space": far * 2 + side}, device_id_type=MESH,
        )

    for side in range(2):
        lanes = slice(side * q_blk, (side + 1) * q_blk)
        part[side, pl.ds(0, ch + 8), :] = acc_far[pl.ds(0, ch + 8), lanes]
        part[side, pl.ds(ch + 8, 8), :] = jnp.broadcast_to(top_far[:, lanes], (8, q_blk))
        part_copy(side).start()
    acc[...] = jnp.zeros_like(acc)

    @pl.loop(0, 2)
    def _(j):
        weigh(odd, acc, pl.multiple_of(j * step_last, step_last), step_last, top_sib)

    sib_out[...] = acc[pl.ds(0, ch), :].astype(SIB)
    sib_facts[pl.ds(0, 8), :] = acc[pl.ds(ch, 8), :]
    sib_facts[pl.ds(8, 8), :] = jnp.broadcast_to(top_sib, (8, q_blk))
    sib_copies = [
        pltpu.make_async_remote_copy(
            a, b, sib_send.at[i], sib_recv.at[i], device_id={"space": sib}, device_id_type=MESH
        )
        for i, (a, b) in enumerate([(sib_out, sib_in), (sib_facts, sib_facts_in)])
    ]
    for copy in sib_copies:
        copy.start()
    for side in range(2):
        part_arrival(side).wait_recv()
    for copy in sib_copies:
        copy.wait_recv()
    parts = [part[2], part_in[0], part_in[1]]
    parts.append(jnp.concatenate([sib_in[...].astype(F32), sib_facts_in[...]], axis=0))
    tops = [p[ch + 8 : ch + 9] for p in parts]
    best = functools.reduce(jnp.maximum, tops)
    mixed = None
    for p, m in zip(parts, tops):
        v = p[: ch + 8] * jnp.exp2((m - best) * scale)
        mixed = v if mixed is None else mixed + v
    inverse = 1.0 / mixed[ch : ch + 1]
    position = mixed[ch + 1 : ch + 3] * inverse
    unit = jnp.where(
        lax.broadcasted_iota(jnp.int32, (2, q_blk), 0) == 0, 1.0 / width, 1.0 / height
    )
    position = position * unit
    att = (mixed[:ch] * inverse).astype(BF16)
    att_own[...] = att

    def halo(side):
        to = lax.rem(t + (1 if side == 0 else n_tm - 1), n_tm)
        return pltpu.make_async_remote_copy(
            att_own, att_in.at[side], halo_send.at[side], halo_recv.at[side],
            device_id={"tm": to}, device_id_type=MESH,
        )

    halo(0).start()
    halo(1).start()
    att = att.astype(F32)
    mid = att * tap_cols[1]
    halo(0).wait_recv()
    halo(1).wait_recv()
    before = jnp.where(t > 0, att_in[0].astype(F32), 0.0)
    after = jnp.where(t < n_tm - 1, att_in[1].astype(F32), 0.0)
    depth = tap_cols[0] * before + mid + tap_cols[2] * after
    hidden = jax.nn.gelu(depth).astype(BF16)
    refined = att + jnp.dot(pw_t[...], hidden, preferred_element_type=F32)
    terms = jnp.dot(
        proj[...].reshape(2 * n_tm, ch), refined, preferred_element_type=F32,
        precision=lax.Precision.HIGHEST,
    )
    term[...] = terms.reshape(n_tm, 2, q_blk)

    own = term[t] + position
    term[t] = own
    term_in[t, y] = own

    def term_copy(r, k):
        return pltpu.make_async_remote_copy(
            term.at[t + r], term_in.at[t, y], term_send.at[r], term_recv.at[t],
            device_id={"tm": t + r, "space": lax.rem(y + k, n_sp)}, device_id_type=MESH,
        )

    def terms_of(source, count, slot):
        some = term_in.at[source, pl.ds(0, count)]
        return pltpu.make_async_remote_copy(
            some, some, term_send.at[slot], term_recv.at[source],
            device_id={"space": lax.rem(y + 1, n_sp)}, device_id_type=MESH,
        )

    for k in range(1, n_sp):
        term_copy(0, k).start()
    for r in range(1, n_tm):

        @pl.when(t + r < n_tm)
        def _():
            for k in range(n_sp):
                term_copy(r, k).start()

    for source in range(n_tm - 1):

        @pl.when(source < t)
        def _():
            terms_of(source, n_sp, 0).wait_recv()

    terms_of(t, n_sp - 1, 0).wait()
    for b in range(n_sp):
        track = term_in[t, b]
        for source in range(n_tm - 1):
            track = track + jnp.where(source < t, term_in[source, b], 0.0)
        out[:, b * q_blk : (b + 1) * q_blk] = track

    all_rs.wait_send()
    all_z.wait_send()
    all_ag.wait_send()
    on_chip.wait_send()
    for side in range(2):
        part_copy(side).wait_send()
    for copy in sib_copies:
        copy.wait_send()
    halo(0).wait_send()
    halo(1).wait_send()
    for r in range(1, n_tm):

        @pl.when(t + r < n_tm)
        def _():
            terms_of(0, n_sp, r).wait_send()


def solution(mesh):
    n_tm, n_sp = mesh.shape["tm"], mesh.shape["space"]

    def local(fm, q_frame, q_row, q_col, decay, taps, pw, out_w):
        frames, rows, width, ch = fm.shape
        n_q = q_frame.shape[0]
        n_pos = rows * width
        plane = 2 * n_sp
        n_z = n_tm // 2
        home = n_q // plane
        q_blk = n_q // n_sp
        half = n_q // 2
        dims = (n_tm, n_sp, n_q, rows, width, ch, rows * n_sp)
        vmem = pl.BlockSpec(memory_space=pltpu.VMEM)
        dma = pltpu.SemaphoreType.DMA
        queries = [a.reshape(n_q // 128, 128) for a in (q_frame, q_row, q_col)]
        out = pl.pallas_call(
            functools.partial(kernel, dims),
            out_shape=pltpu.VMEM((2, n_q), F32),
            in_specs=[pl.BlockSpec(memory_space=pl.ANY)] + [vmem] * 7,
            out_specs=vmem,
            scratch_shapes=[
                pltpu.VMEM((n_q // 128, 128), jnp.int32),
                pltpu.SMEM((n_q // 128, 128), jnp.int32),
                pltpu.VMEM((n_pos, ch), BF16),
                pltpu.VMEM((n_pos + 8, ch), F32),
                pltpu.VMEM((ch + 16, n_pos), BF16),
                pltpu.VMEM((n_q, ch), F32),
                pltpu.VMEM((plane, home, ch), BF16),
                pltpu.VMEM((plane - 1, home, ch), BF16),
                pltpu.VMEM((home, ch), BF16),
                pltpu.VMEM((n_z - 1, home, ch), BF16),
                pltpu.VMEM((home, ch), BF16),
                pltpu.VMEM((plane, home, ch), BF16),
                pltpu.VMEM((ch, half), BF16),
                pltpu.VMEM((ch, q_blk), BF16),
                pltpu.VMEM((n_tm, 1, ch), F32),
                pltpu.VMEM((3, ch, q_blk), F32),
                pltpu.VMEM((ch, ch), BF16),
                pltpu.VMEM((n_tm, 2, ch), F32),
                pltpu.VMEM((n_pos, half), F32),
                pltpu.VMEM((n_pos, q_blk), F32),
                pltpu.VMEM((ch + 16, half), F32),
                pltpu.VMEM((ch + 16, q_blk), F32),
                pltpu.VMEM((3, ch + 16, q_blk), F32),
                pltpu.VMEM((2, ch + 16, q_blk), F32),
                pltpu.VMEM((ch, q_blk), SIB),
                pltpu.VMEM((ch, q_blk), SIB),
                pltpu.VMEM((16, q_blk), F32),
                pltpu.VMEM((16, q_blk), F32),
                pltpu.VMEM((ch, q_blk), BF16),
                pltpu.VMEM((2, ch, q_blk), BF16),
                pltpu.VMEM((n_tm, 2, q_blk), F32),
                pltpu.VMEM((n_tm, n_sp, 2, q_blk), F32),
                dma((4,)), dma, dma, dma, dma, dma, dma, dma, dma, dma, dma, dma,
                dma((2,)), dma((2,)), dma((2,)), dma((2,)), dma((2,)), dma((2,)),
                dma((n_tm,)), dma((n_tm,)),
            ],
            compiler_params=pltpu.CompilerParams(collective_id=0, has_side_effects=True),
        )(fm.reshape(n_pos, ch), *queries, decay, taps, pw, out_w)
        return out[None]

    placed = (
        P(("video", "tm"), "space", None, None),
        P("video"),
        P("video"),
        P("video"),
        P(("video", "tm"), None),
        P(),
        P(),
        P(),
    )
    return jax.shard_map(
        local, mesh=mesh, in_specs=placed, out_specs=P(("video", "tm"), None, None), check_vma=False
    )
```

```python
import functools
import math

import jax
import jax.numpy as jnp
from jax import lax
from jax.experimental import pallas as pl
from jax.experimental.pallas import tpu as pltpu
from jax.sharding import PartitionSpec as P

MESH = pl.DeviceIdType.MESH
F32 = jnp.float32
BF16 = jnp.bfloat16


def far_first(n):
    return sorted(range(1, n), key=lambda r: -min(r, n - r))


def kernel(
    dims, fm, q_frame, q_row, q_col, decay_hbm, taps_hbm, pw_hbm, out_w_hbm, out,
    asked, decay, taps, pw, out_w, rows_v, rows_s, keys, keys32, keys_t, contrib32, contrib, rs_in, z_own, z_in, q_own, q_all, q_far, q_near, decay_all,
    tap_cols, pw_t, proj, even, odd, acc_far, acc, own_part, feats, feats_in, facts, facts_in, att_own, att_in, term, term_in,
    ask_sem, small_sem, key_sem, row_sem, rs_send, rs_recv, z_send, z_recv, ag_send, ag_recv, on_send,
    on_recv, dec_send, dec_recv,
    feat_send, feat_recv, fact_send, fact_recv, halo_send, halo_recv, term_send, term_recv,
):
    n_tm, n_sp, n_q, rows, width, ch, height = dims
    n_z = n_tm // 2
    plane = 2 * n_sp
    q_blk = n_q // n_sp
    n_pos = rows * width
    t = lax.axis_index("tm")
    y = lax.axis_index("space")
    z = lax.div(t, 2)
    core = lax.rem(t, 2)
    me = y * 2 + core

    def in_plane(r):
        other = lax.rem(me + r, plane)
        return other, {"tm": z * 2 + lax.rem(other, 2), "space": lax.div(other, 2)}

    def along_z(r):
        return {"tm": lax.rem(t + 2 * r, n_tm)}

    n_loads = 4
    piece = n_pos // n_loads

    def load(i):
        cut = pl.ds(i * piece, piece)
        return pltpu.make_async_copy(fm.at[cut], keys.at[cut], key_sem.at[i])

    asks = [
        pltpu.make_async_copy(a, asked.at[i], ask_sem.at[i])
        for i, a in enumerate([q_frame, q_row, q_col])
    ]
    smalls = [
        pltpu.make_async_copy(a, b, small_sem.at[i])
        for i, (a, b) in enumerate(
            [(decay_hbm, decay), (taps_hbm, taps), (pw_hbm, pw), (out_w_hbm, out_w)]
        )
    ]
    for copy in asks:
        copy.start()
    for i in range(n_loads):
        load(i).start()
    for copy in smalls:
        copy.start()
    barrier = pltpu.get_barrier_semaphore()
    for r in range(1, n_tm):
        pl.semaphore_signal(
            barrier, inc=1, device_id={"tm": lax.rem(t + r, n_tm)}, device_id_type=MESH
        )
    for r in range(1, n_sp):
        for c in range(2):
            pl.semaphore_signal(
                barrier, inc=1, device_id={"tm": z * 2 + c, "space": lax.rem(y + r, n_sp)},
                device_id_type=MESH,
            )
    for copy in asks:
        copy.wait()
    line = asked[0] * height + asked[1] - (t * height + y * rows)
    mine = (line >= 0) & (line < rows)
    rows_v[...] = jnp.where(mine, line * width + asked[2], n_pos)
    tell = pltpu.make_async_copy(rows_v, rows_s, row_sem)
    tell.start()
    step = 384
    keys32[pl.ds(n_pos, 8), :] = jnp.zeros((8, ch), F32)
    for i in range(n_loads):
        load(i).wait()

        @pl.loop(0, piece // step)
        def _(j):
            at = pl.multiple_of(i * piece + j * step, step)
            keys32[pl.ds(at, step), :] = keys[pl.ds(at, step), :].astype(F32)

    tell.wait()
    homes = plane // n_sp

    def rs_sends(k):
        for c in range(homes):
            block = lax.rem(y + k, n_sp)
            there = lax.rem(2 * (n_sp - k) + core - c + plane, plane) - 1

            @pl.when(there >= 0)
            def _():
                pltpu.make_async_remote_copy(
                    contrib.at[block * 2 + c], rs_in.at[there], rs_send, rs_recv,
                    device_id={"tm": z * 2 + c, "space": block}, device_id_type=MESH,
                ).start()

    order = far_first(n_sp) + [0]
    for i, k in enumerate(order):
        block = lax.rem(y + k, n_sp)
        first = pl.multiple_of(block * q_blk, q_blk)

        @pl.loop(0, q_blk // 16)
        def _(j):
            for u in range(16):
                at = rows_s[block, j * 16 + u]
                contrib32[pl.ds(first + j * 16 + u, 1), :] = keys32[pl.ds(at, 1), :]

        contrib[pl.ds(block * 2, 2)] = (
            contrib32[pl.ds(first, q_blk), :].reshape(2, q_blk // 2, ch).astype(BF16)
        )
        if i == 0:
            pl.semaphore_wait(barrier, n_tm - 1 + plane - 2)
            for past in order[:i]:
                rs_sends(past)
        if i >= 0:
            rs_sends(k)

    for copy in smalls:
        copy.wait()
    decay_all[t] = decay[...]

    @pl.loop(1, n_tm)
    def _(r):
        pltpu.make_async_remote_copy(
            decay, decay_all.at[t], dec_send, dec_recv,
            device_id={"tm": lax.rem(t + r, n_tm)}, device_id_type=MESH,
        ).start()

    all_rs = pltpu.make_async_remote_copy(
        rs_in, rs_in, rs_send, rs_recv, device_id=in_plane(1)[1], device_id_type=MESH
    )
    all_rs.wait_recv()
    total = contrib[me].astype(F32) + jnp.sum(rs_in[...].astype(F32), axis=0)
    z_own[...] = total.astype(BF16)
    for r in far_first(n_z):
        pltpu.make_async_remote_copy(
            z_own, z_in.at[r - 1], z_send, z_recv, device_id=along_z(r), device_id_type=MESH
        ).start()

    @pl.loop(0, n_pos // 128)
    def _(j):
        at = pl.multiple_of(j * 128, 128)
        keys_t[pl.ds(0, ch), pl.ds(at, 128)] = keys32[pl.ds(at, 128), :].T.astype(BF16)

    place = lax.broadcasted_iota(jnp.int32, (16, n_pos), 1).astype(F32)
    line = jnp.floor((place + 0.5) * (1.0 / width))
    col = place - line * width
    line = line + (y * rows).astype(F32)
    kind = lax.broadcasted_iota(jnp.int32, (16, n_pos), 0)
    extra = jnp.where(kind == 0, 1.0, jnp.where(kind == 1, col, jnp.where(kind == 2, line, 0.0)))
    keys_t[pl.ds(ch, 16), :] = extra.astype(BF16)

    all_z = pltpu.make_async_remote_copy(
        z_in, z_in, z_send, z_recv, device_id=along_z(1), device_id_type=MESH
    )
    all_z.wait_recv()
    total = total + jnp.sum(z_in[...].astype(F32), axis=0)
    q_own[...] = total.astype(BF16)
    q_all[me] = total.astype(BF16)
    on_chip = pltpu.make_async_remote_copy(
        q_own, q_all.at[me], on_send, on_recv, device_id={"tm": t + 1 - 2 * core},
        device_id_type=MESH,
    )
    on_chip.start()
    for k in (1, 3, 2):
        for c in range(2):
            pltpu.make_async_remote_copy(
                q_own, q_all.at[me], ag_send.at[k % 2], ag_recv.at[k % 2],
                device_id={"tm": z * 2 + c, "space": lax.rem(y + k, n_sp)}, device_id_type=MESH,
            ).start()

    odd_row = lax.rem(y, 2)
    scale = math.log2(math.e) / math.sqrt(ch)

    def turned(first, count):
        return q_all[pl.ds(first, count)].astype(F32).reshape(-1, ch).T.astype(BF16)

    def score(buf, q, at, size):
        s = jnp.dot(keys[pl.ds(at, size), :], q[...], preferred_element_type=F32)
        buf[pl.ds(at, size), :] = s
        return jnp.max(s.reshape(size // 8, 8, s.shape[1]), axis=0)

    def weigh(buf, total, at, size, top):
        e = jnp.exp2((buf[pl.ds(at, size), :] - top) * scale).astype(BF16)
        total[...] += jnp.dot(keys_t[:, pl.ds(at, size)], e, preferred_element_type=F32)

    step_both, step_last = n_pos // 3, n_pos // 2

    on_chip.wait_recv()
    q_near[...] = turned(2 * y, 2)
    top_own = jnp.max(score(odd, q_near, 0, n_pos), axis=0, keepdims=True)
    acc[...] = jnp.zeros_like(acc)

    @pl.loop(0, 2)
    def _(j):
        weigh(odd, acc, pl.multiple_of(j * step_last, step_last), step_last, top_own)

    own_part[...] = acc[pl.ds(0, ch + 8), :]

    eye = lax.broadcasted_iota(jnp.int32, (ch, ch), 0) == lax.broadcasted_iota(
        jnp.int32, (ch, ch), 1
    )
    for k in range(3):
        column = jnp.sum(jnp.where(eye, taps[pl.ds(k, 1), :], 0.0), axis=1, keepdims=True)
        tap_cols[k] = jnp.broadcast_to(column, (ch, q_blk))
    pw_t[...] = pw[...].astype(F32).T.astype(BF16)
    all_dec = pltpu.make_async_remote_copy(
        decay_all.at[pl.ds(0, n_tm - 1)], decay_all.at[pl.ds(0, n_tm - 1)], dec_send, dec_recv,
        device_id={"tm": lax.rem(t + 1, n_tm)}, device_id_type=MESH,
    )
    all_dec.wait()
    run = out_w[...] * (1.0 - decay[...])
    gain = jnp.zeros_like(run)
    for frame in range(n_tm):
        kept = gain if frame == 0 else gain * decay_all[frame]
        gain = jnp.where(t == frame, run, jnp.where(t < frame, kept, 0.0))
        proj[frame] = gain

    def ag_of(k):
        some = q_all.at[pl.ds(0, 2 + 2 * k)]
        return pltpu.make_async_remote_copy(
            some, some, ag_send.at[k], ag_recv.at[k],
            device_id=in_plane(1)[1], device_id_type=MESH,
        )

    ag_of(1).wait_recv()
    sib = lax.rem(y + 2, n_sp)
    for side in range(2):
        lanes = slice(side * q_blk, (side + 1) * q_blk)
        q_far[:, lanes] = turned(2 * (1 - odd_row) + 4 * side, 2)
    top_far = jnp.max(score(even, q_far, 0, n_pos), axis=0, keepdims=True)
    acc_far[...] = jnp.zeros_like(acc_far)
    ag_of(0).wait_recv()
    q_near[...] = turned(2 * sib, 2)

    def both(j, top):
        at = pl.multiple_of(j * step_both, step_both)
        top = jnp.maximum(top, score(odd, q_near, at, step_both))
        weigh(even, acc_far, at, step_both, top_far)
        return top

    top_sib = lax.fori_loop(0, 3, both, jnp.full((8, q_blk), -jnp.inf, F32))
    top_sib = jnp.max(top_sib, axis=0, keepdims=True)

    def hand_over(slot, to, there, sums, top):
        feats[slot] = sums[:ch].astype(BF16)
        facts[slot, pl.ds(0, 8), :] = sums[ch:]
        facts[slot, pl.ds(8, 8), :] = jnp.broadcast_to(top, (8, q_blk))
        for copy in part_copies(slot, to, there):
            copy.start()

    def part_copies(slot, to, there):
        return [
            pltpu.make_async_remote_copy(
                source.at[slot], target.at[there], send.at[slot], recv.at[there],
                device_id={"space": to}, device_id_type=MESH,
            )
            for source, target, send, recv in [
                (facts, facts_in, fact_send, fact_recv), (feats, feats_in, feat_send, feat_recv)
            ]
        ]

    for side in range(2):
        lanes = slice(side * q_blk, (side + 1) * q_blk)
        hand_over(
            side, 1 - odd_row + 2 * side, lax.div(y, 2), acc_far[pl.ds(0, ch + 8), lanes],
            top_far[:, lanes],
        )
    acc[...] = jnp.zeros_like(acc)

    @pl.loop(0, 2)
    def _(j):
        weigh(odd, acc, pl.multiple_of(j * step_last, step_last), step_last, top_sib)

    hand_over(2, sib, 2, acc[pl.ds(0, ch + 8), :], top_sib)
    parts = [(own_part[...], top_own)]
    for slot in range(3):
        for copy in part_copies(slot, sib, slot):
            copy.wait_recv()
    for slot in range(3):
        sums = jnp.concatenate([feats_in[slot].astype(F32), facts_in[slot, pl.ds(0, 8), :]], axis=0)
        parts.append((sums, facts_in[slot, pl.ds(8, 1), :]))
    best = functools.reduce(jnp.maximum, [top for _, top in parts])
    mixed = None
    for sums, top in parts:
        v = sums * jnp.exp2((top - best) * scale)
        mixed = v if mixed is None else mixed + v
    inverse = 1.0 / mixed[ch : ch + 1]
    position = mixed[ch + 1 : ch + 3] * inverse
    unit = jnp.where(
        lax.broadcasted_iota(jnp.int32, (2, q_blk), 0) == 0, 1.0 / width, 1.0 / height
    )
    position = position * unit
    att = (mixed[:ch] * inverse).astype(BF16)
    att_own[...] = att

    def halo(side):
        to = lax.rem(t + (1 if side == 0 else n_tm - 1), n_tm)
        return pltpu.make_async_remote_copy(
            att_own, att_in.at[side], halo_send.at[side], halo_recv.at[side],
            device_id={"tm": to}, device_id_type=MESH,
        )

    halo(0).start()
    halo(1).start()
    att = att.astype(F32)
    mid = att * tap_cols[1]
    halo(0).wait_recv()
    halo(1).wait_recv()
    before = jnp.where(t > 0, att_in[0].astype(F32), 0.0)
    after = jnp.where(t < n_tm - 1, att_in[1].astype(F32), 0.0)
    depth = tap_cols[0] * before + mid + tap_cols[2] * after
    hidden = jax.nn.gelu(depth).astype(BF16)
    refined = att + jnp.dot(pw_t[...], hidden, preferred_element_type=F32)
    terms = jnp.dot(
        proj[...].reshape(2 * n_tm, ch), refined, preferred_element_type=F32,
        precision=lax.Precision.HIGHEST,
    )
    term[...] = terms.reshape(n_tm, 2, q_blk)

    own = term[t] + position
    term[t] = own
    term_in[t, y] = own

    def term_copy(r, k):
        return pltpu.make_async_remote_copy(
            term.at[t + r], term_in.at[t, y], term_send.at[r], term_recv.at[t],
            device_id={"tm": t + r, "space": lax.rem(y + k, n_sp)}, device_id_type=MESH,
        )

    def terms_of(source, count, slot):
        some = term_in.at[source, pl.ds(0, count)]
        return pltpu.make_async_remote_copy(
            some, some, term_send.at[slot], term_recv.at[source],
            device_id={"space": lax.rem(y + 1, n_sp)}, device_id_type=MESH,
        )

    for k in range(1, n_sp):
        term_copy(0, k).start()
    for r in range(1, n_tm):

        @pl.when(t + r < n_tm)
        def _():
            for k in range(n_sp):
                term_copy(r, k).start()

    for source in range(n_tm - 1):

        @pl.when(source < t)
        def _():
            terms_of(source, n_sp, 0).wait_recv()

    terms_of(t, n_sp - 1, 0).wait()
    for b in range(n_sp):
        track = term_in[t, b]
        for source in range(n_tm - 1):
            track = track + jnp.where(source < t, term_in[source, b], 0.0)
        out[:, b * q_blk : (b + 1) * q_blk] = track

    all_rs.wait_send()
    all_z.wait_send()
    ag_of(0).wait_send()
    ag_of(1).wait_send()
    on_chip.wait_send()
    for slot in range(3):
        for copy in part_copies(slot, sib, slot):
            copy.wait_send()
    halo(0).wait_send()
    halo(1).wait_send()
    for r in range(1, n_tm):

        @pl.when(t + r < n_tm)
        def _():
            terms_of(0, n_sp, r).wait_send()


def solution(mesh):
    n_tm, n_sp = mesh.shape["tm"], mesh.shape["space"]

    def local(fm, q_frame, q_row, q_col, decay, taps, pw, out_w):
        frames, rows, width, ch = fm.shape
        n_q = q_frame.shape[0]
        n_pos = rows * width
        plane = 2 * n_sp
        n_z = n_tm // 2
        home = n_q // plane
        q_blk = n_q // n_sp
        half = n_q // 2
        dims = (n_tm, n_sp, n_q, rows, width, ch, rows * n_sp)
        vmem = pl.BlockSpec(memory_space=pltpu.VMEM)
        dma = pltpu.SemaphoreType.DMA
        queries = [a.reshape(n_q // 128, 128) for a in (q_frame, q_row, q_col)]
        out = pl.pallas_call(
            functools.partial(kernel, dims),
            out_shape=pltpu.VMEM((2, n_q), F32),
            in_specs=[pl.BlockSpec(memory_space=pl.ANY)] * 8,
            out_specs=vmem,
            scratch_shapes=[
                pltpu.VMEM((3, n_q // 128, 128), jnp.int32),
                pltpu.VMEM(decay.shape, F32),
                pltpu.VMEM(taps.shape, F32),
                pltpu.VMEM(pw.shape, BF16),
                pltpu.VMEM(out_w.shape, F32),
                pltpu.VMEM((n_q // 128, 128), jnp.int32),
                pltpu.SMEM((n_q // 128, 128), jnp.int32),
                pltpu.VMEM((n_pos, ch), BF16),
                pltpu.VMEM((n_pos + 8, ch), F32),
                pltpu.VMEM((ch + 16, n_pos), BF16),
                pltpu.VMEM((n_q, ch), F32),
                pltpu.VMEM((plane, home, ch), BF16),
                pltpu.VMEM((plane - 1, home, ch), BF16),
                pltpu.VMEM((home, ch), BF16),
                pltpu.VMEM((n_z - 1, home, ch), BF16),
                pltpu.VMEM((home, ch), BF16),
                pltpu.VMEM((plane, home, ch), BF16),
                pltpu.VMEM((ch, half), BF16),
                pltpu.VMEM((ch, q_blk), BF16),
                pltpu.VMEM((n_tm, 1, ch), F32),
                pltpu.VMEM((3, ch, q_blk), F32),
                pltpu.VMEM((ch, ch), BF16),
                pltpu.VMEM((n_tm, 2, ch), F32),
                pltpu.VMEM((n_pos, half), F32),
                pltpu.VMEM((n_pos, q_blk), F32),
                pltpu.VMEM((ch + 16, half), F32),
                pltpu.VMEM((ch + 16, q_blk), F32),
                pltpu.VMEM((ch + 8, q_blk), F32),
                pltpu.VMEM((3, ch, q_blk), BF16),
                pltpu.VMEM((3, ch, q_blk), BF16),
                pltpu.VMEM((3, 16, q_blk), F32),
                pltpu.VMEM((3, 16, q_blk), F32),
                pltpu.VMEM((ch, q_blk), BF16),
                pltpu.VMEM((2, ch, q_blk), BF16),
                pltpu.VMEM((n_tm, 2, q_blk), F32),
                pltpu.VMEM((n_tm, n_sp, 2, q_blk), F32),
                dma((3,)), dma((4,)), dma((4,)), dma, dma, dma, dma, dma, dma((2,)), dma((2,)), dma, dma, dma, dma,
                dma((3,)), dma((3,)), dma((3,)), dma((3,)), dma((2,)), dma((2,)),
                dma((n_tm,)), dma((n_tm,)),
            ],
            compiler_params=pltpu.CompilerParams(collective_id=0, has_side_effects=True),
        )(fm.reshape(n_pos, ch), *queries, decay, taps, pw, out_w)
        return out[None]

    placed = (
        P(("video", "tm"), "space", None, None),
        P("video"),
        P("video"),
        P("video"),
        P(("video", "tm"), None),
        P(),
        P(),
        P(),
    )
    return jax.shard_map(
        local, mesh=mesh, in_specs=placed, out_specs=P(("video", "tm"), None, None), check_vma=False
    )
```

```python
import functools
import math

import jax
import jax.numpy as jnp
from jax import lax
from jax.experimental import pallas as pl
from jax.experimental.pallas import tpu as pltpu
from jax.sharding import PartitionSpec as P

MESH = pl.DeviceIdType.MESH
F32 = jnp.float32
BF16 = jnp.bfloat16


def far_first(n):
    return sorted(range(1, n), key=lambda r: -min(r, n - r))


def kernel(
    dims, fm, q_frame, q_row, q_col, decay_hbm, taps_hbm, pw_hbm, out_w_hbm, out,
    asked, decay, taps, pw, out_w, rows_v, rows_s, keys, keys32, keys_t, contrib32, contrib, rs_in, z_own, z_in, q_own, q_all, q_far, q_near, decay_all,
    tap_cols, pw_t, proj, even, odd, acc_far, acc, own_part, feats, feats_in, facts, facts_in, att_own, att_in, term, term_in,
    ask_sem, small_sem, key_sem, row_sem, rs_send, rs_recv, z_send, z_recv, ag_send, ag_recv, on_send,
    on_recv, dec_send, dec_recv,
    feat_send, feat_recv, fact_send, fact_recv, halo_send, halo_recv, term_send, term_recv,
):
    n_tm, n_sp, n_q, rows, width, ch, height = dims
    n_z = n_tm // 2
    plane = 2 * n_sp
    q_blk = n_q // n_sp
    n_pos = rows * width
    t = lax.axis_index("tm")
    y = lax.axis_index("space")
    z = lax.div(t, 2)
    core = lax.rem(t, 2)
    me = y * 2 + core

    def in_plane(r):
        other = lax.rem(me + r, plane)
        return other, {"tm": z * 2 + lax.rem(other, 2), "space": lax.div(other, 2)}

    def along_z(r):
        return {"tm": lax.rem(t + 2 * r, n_tm)}

    n_loads = 4
    piece = n_pos // n_loads

    def load(i):
        cut = pl.ds(i * piece, piece)
        return pltpu.make_async_copy(fm.at[cut], keys.at[cut], key_sem.at[i])

    asks = [
        pltpu.make_async_copy(a, asked.at[i], ask_sem.at[i])
        for i, a in enumerate([q_frame, q_row, q_col])
    ]
    smalls = [
        pltpu.make_async_copy(a, b, small_sem.at[i])
        for i, (a, b) in enumerate(
            [(decay_hbm, decay), (taps_hbm, taps), (pw_hbm, pw), (out_w_hbm, out_w)]
        )
    ]
    for copy in asks:
        copy.start()
    for i in range(n_loads):
        load(i).start()
    for copy in smalls:
        copy.start()
    barrier = pltpu.get_barrier_semaphore()
    for r in range(1, n_tm):
        pl.semaphore_signal(
            barrier, inc=1, device_id={"tm": lax.rem(t + r, n_tm)}, device_id_type=MESH
        )
    for r in range(1, n_sp):
        for c in range(2):
            pl.semaphore_signal(
                barrier, inc=1, device_id={"tm": z * 2 + c, "space": lax.rem(y + r, n_sp)},
                device_id_type=MESH,
            )
    for copy in asks:
        copy.wait()
    line = asked[0] * height + asked[1] - (t * height + y * rows)
    mine = (line >= 0) & (line < rows)
    rows_v[...] = jnp.where(mine, line * width + asked[2], n_pos)
    tell = pltpu.make_async_copy(rows_v, rows_s, row_sem)
    tell.start()
    step = 384
    keys32[pl.ds(n_pos, 8), :] = jnp.zeros((8, ch), F32)
    for i in range(n_loads):
        load(i).wait()

        @pl.loop(0, piece // step)
        def _(j):
            at = pl.multiple_of(i * piece + j * step, step)
            keys32[pl.ds(at, step), :] = keys[pl.ds(at, step), :].astype(F32)

    tell.wait()
    homes = plane // n_sp

    def rs_sends(k):
        for c in range(homes):
            block = lax.rem(y + k, n_sp)
            there = lax.rem(2 * (n_sp - k) + core - c + plane, plane) - 1

            @pl.when(there >= 0)
            def _():
                pltpu.make_async_remote_copy(
                    contrib.at[block * 2 + c], rs_in.at[there], rs_send, rs_recv,
                    device_id={"tm": z * 2 + c, "space": block}, device_id_type=MESH,
                ).start()

    @pl.loop(0, n_sp)
    def _(i):
        k = jnp.where(i == 0, 2, jnp.where(i == 1, 1, jnp.where(i == 2, 3, 0)))
        block = lax.rem(y + k, n_sp)
        first = pl.multiple_of(block * q_blk, q_blk)
        for u in range(q_blk):
            at = rows_s[block, u]
            contrib32[pl.ds(first + u, 1), :] = keys32[pl.ds(at, 1), :]
        contrib[pl.ds(block * 2, 2)] = (
            contrib32[pl.ds(first, q_blk), :].reshape(2, q_blk // 2, ch).astype(BF16)
        )

    pl.semaphore_wait(barrier, n_tm - 1 + plane - 2)
    for k in far_first(n_sp) + [0]:
        rs_sends(k)

    for copy in smalls:
        copy.wait()
    decay_all[t] = decay[...]

    @pl.loop(1, n_tm)
    def _(r):
        pltpu.make_async_remote_copy(
            decay, decay_all.at[t], dec_send, dec_recv,
            device_id={"tm": lax.rem(t + r, n_tm)}, device_id_type=MESH,
        ).start()

    all_rs = pltpu.make_async_remote_copy(
        rs_in, rs_in, rs_send, rs_recv, device_id=in_plane(1)[1], device_id_type=MESH
    )
    all_rs.wait_recv()
    total = contrib[me].astype(F32) + jnp.sum(rs_in[...].astype(F32), axis=0)
    z_own[...] = total.astype(BF16)
    for r in far_first(n_z):
        pltpu.make_async_remote_copy(
            z_own, z_in.at[r - 1], z_send, z_recv, device_id=along_z(r), device_id_type=MESH
        ).start()

    @pl.loop(0, n_pos // 128)
    def _(j):
        at = pl.multiple_of(j * 128, 128)
        keys_t[pl.ds(0, ch), pl.ds(at, 128)] = keys32[pl.ds(at, 128), :].T.astype(BF16)

    place = lax.broadcasted_iota(jnp.int32, (16, n_pos), 1).astype(F32)
    line = jnp.floor((place + 0.5) * (1.0 / width))
    col = place - line * width
    line = line + (y * rows).astype(F32)
    kind = lax.broadcasted_iota(jnp.int32, (16, n_pos), 0)
    extra = jnp.where(kind == 0, 1.0, jnp.where(kind == 1, col, jnp.where(kind == 2, line, 0.0)))
    keys_t[pl.ds(ch, 16), :] = extra.astype(BF16)

    all_z = pltpu.make_async_remote_copy(
        z_in, z_in, z_send, z_recv, device_id=along_z(1), device_id_type=MESH
    )
    all_z.wait_recv()
    total = total + jnp.sum(z_in[...].astype(F32), axis=0)
    q_own[...] = total.astype(BF16)
    q_all[me] = total.astype(BF16)
    on_chip = pltpu.make_async_remote_copy(
        q_own, q_all.at[me], on_send, on_recv, device_id={"tm": t + 1 - 2 * core},
        device_id_type=MESH,
    )
    on_chip.start()
    for k in (1, 3, 2):
        for c in range(2):
            pltpu.make_async_remote_copy(
                q_own, q_all.at[me], ag_send.at[k % 2], ag_recv.at[k % 2],
                device_id={"tm": z * 2 + c, "space": lax.rem(y + k, n_sp)}, device_id_type=MESH,
            ).start()

    odd_row = lax.rem(y, 2)
    scale = math.log2(math.e) / math.sqrt(ch)

    def turned(first, count):
        return q_all[pl.ds(first, count)].astype(F32).reshape(-1, ch).T.astype(BF16)

    def score(buf, q, at, size):
        s = jnp.dot(keys[pl.ds(at, size), :], q[...], preferred_element_type=F32)
        buf[pl.ds(at, size), :] = s
        return jnp.max(s.reshape(size // 8, 8, s.shape[1]), axis=0)

    def weigh(buf, total, at, size, top):
        e = jnp.exp2((buf[pl.ds(at, size), :] - top) * scale).astype(BF16)
        total[...] += jnp.dot(keys_t[:, pl.ds(at, size)], e, preferred_element_type=F32)

    step_both, step_last = n_pos // 3, n_pos // 2

    on_chip.wait_recv()
    q_near[...] = turned(2 * y, 2)
    top_own = jnp.max(score(odd, q_near, 0, n_pos), axis=0, keepdims=True)
    acc[...] = jnp.zeros_like(acc)

    @pl.loop(0, 2)
    def _(j):
        weigh(odd, acc, pl.multiple_of(j * step_last, step_last), step_last, top_own)

    own_part[...] = acc[pl.ds(0, ch + 8), :]

    eye = lax.broadcasted_iota(jnp.int32, (ch, ch), 0) == lax.broadcasted_iota(
        jnp.int32, (ch, ch), 1
    )
    for k in range(3):
        column = jnp.sum(jnp.where(eye, taps[pl.ds(k, 1), :], 0.0), axis=1, keepdims=True)
        tap_cols[k] = jnp.broadcast_to(column, (ch, q_blk))
    pw_t[...] = pw[...].astype(F32).T.astype(BF16)
    all_dec = pltpu.make_async_remote_copy(
        decay_all.at[pl.ds(0, n_tm - 1)], decay_all.at[pl.ds(0, n_tm - 1)], dec_send, dec_recv,
        device_id={"tm": lax.rem(t + 1, n_tm)}, device_id_type=MESH,
    )
    all_dec.wait()
    run = out_w[...] * (1.0 - decay[...])
    gain = jnp.zeros_like(run)
    for frame in range(n_tm):
        kept = gain if frame == 0 else gain * decay_all[frame]
        gain = jnp.where(t == frame, run, jnp.where(t < frame, kept, 0.0))
        proj[frame] = gain

    def ag_of(k):
        some = q_all.at[pl.ds(0, 2 + 2 * k)]
        return pltpu.make_async_remote_copy(
            some, some, ag_send.at[k], ag_recv.at[k],
            device_id=in_plane(1)[1], device_id_type=MESH,
        )

    ag_of(1).wait_recv()
    sib = lax.rem(y + 2, n_sp)
    for side in range(2):
        lanes = slice(side * q_blk, (side + 1) * q_blk)
        q_far[:, lanes] = turned(2 * (1 - odd_row) + 4 * side, 2)
    top_far = jnp.max(score(even, q_far, 0, n_pos), axis=0, keepdims=True)
    acc_far[...] = jnp.zeros_like(acc_far)
    ag_of(0).wait_recv()
    q_near[...] = turned(2 * sib, 2)

    def both(j, top):
        at = pl.multiple_of(j * step_both, step_both)
        top = jnp.maximum(top, score(odd, q_near, at, step_both))
        weigh(even, acc_far, at, step_both, top_far)
        return top

    top_sib = lax.fori_loop(0, 3, both, jnp.full((8, q_blk), -jnp.inf, F32))
    top_sib = jnp.max(top_sib, axis=0, keepdims=True)

    def hand_over(slot, to, there, sums, top):
        feats[slot] = sums[:ch].astype(BF16)
        spare = lax.broadcasted_iota(jnp.int32, (8, q_blk), 0) == 3
        facts[slot] = jnp.where(spare, top, sums[ch:])
        for copy in part_copies(slot, to, there):
            copy.start()

    def part_copies(slot, to, there):
        return [
            pltpu.make_async_remote_copy(
                source.at[slot], target.at[there], send.at[slot], recv.at[there],
                device_id={"space": to}, device_id_type=MESH,
            )
            for source, target, send, recv in [
                (facts, facts_in, fact_send, fact_recv), (feats, feats_in, feat_send, feat_recv)
            ]
        ]

    for side in range(2):
        lanes = slice(side * q_blk, (side + 1) * q_blk)
        hand_over(
            side, 1 - odd_row + 2 * side, lax.div(y, 2), acc_far[pl.ds(0, ch + 8), lanes],
            top_far[:, lanes],
        )
    acc[...] = jnp.zeros_like(acc)

    @pl.loop(0, 2)
    def _(j):
        weigh(odd, acc, pl.multiple_of(j * step_last, step_last), step_last, top_sib)

    hand_over(2, sib, 2, acc[pl.ds(0, ch + 8), :], top_sib)
    parts = [(own_part[...], top_own)]
    for slot in range(3):
        for copy in part_copies(slot, sib, slot):
            copy.wait_recv()
    for slot in range(3):
        sums = jnp.concatenate([feats_in[slot].astype(F32), facts_in[slot]], axis=0)
        parts.append((sums, facts_in[slot, pl.ds(3, 1), :]))
    best = functools.reduce(jnp.maximum, [top for _, top in parts])
    mixed = None
    for sums, top in parts:
        v = sums * jnp.exp2((top - best) * scale)
        mixed = v if mixed is None else mixed + v
    inverse = 1.0 / mixed[ch : ch + 1]
    position = mixed[ch + 1 : ch + 3] * inverse
    unit = jnp.where(
        lax.broadcasted_iota(jnp.int32, (2, q_blk), 0) == 0, 1.0 / width, 1.0 / height
    )
    position = position * unit
    att = (mixed[:ch] * inverse).astype(BF16)
    att_own[...] = att

    def halo(side):
        to = lax.rem(t + (1 if side == 0 else n_tm - 1), n_tm)
        return pltpu.make_async_remote_copy(
            att_own, att_in.at[side], halo_send.at[side], halo_recv.at[side],
            device_id={"tm": to}, device_id_type=MESH,
        )

    halo(0).start()
    halo(1).start()
    att = att.astype(F32)
    mid = att * tap_cols[1]
    halo(0).wait_recv()
    halo(1).wait_recv()
    before = jnp.where(t > 0, att_in[0].astype(F32), 0.0)
    after = jnp.where(t < n_tm - 1, att_in[1].astype(F32), 0.0)
    depth = tap_cols[0] * before + mid + tap_cols[2] * after
    hidden = jax.nn.gelu(depth).astype(BF16)
    refined = att + jnp.dot(pw_t[...], hidden, preferred_element_type=F32)
    terms = jnp.dot(
        proj[...].reshape(2 * n_tm, ch), refined, preferred_element_type=F32,
        precision=lax.Precision.HIGHEST,
    )
    term[...] = terms.reshape(n_tm, 2, q_blk)

    own = term[t] + position
    term[t] = own
    term_in[t, y] = own

    def term_copy(r, k):
        return pltpu.make_async_remote_copy(
            term.at[t + r], term_in.at[t, y], term_send.at[r], term_recv.at[t],
            device_id={"tm": t + r, "space": lax.rem(y + k, n_sp)}, device_id_type=MESH,
        )

    def terms_of(source, count, slot):
        some = term_in.at[source, pl.ds(0, count)]
        return pltpu.make_async_remote_copy(
            some, some, term_send.at[slot], term_recv.at[source],
            device_id={"space": lax.rem(y + 1, n_sp)}, device_id_type=MESH,
        )

    for k in range(1, n_sp):
        term_copy(0, k).start()
    for r in range(1, n_tm):

        @pl.when(t + r < n_tm)
        def _():
            for k in range(n_sp):
                term_copy(r, k).start()

    for source in range(n_tm - 1):

        @pl.when(source < t)
        def _():
            terms_of(source, n_sp, 0).wait_recv()

    terms_of(t, n_sp - 1, 0).wait()
    for b in range(n_sp):
        track = term_in[t, b]
        for source in range(n_tm - 1):
            track = track + jnp.where(source < t, term_in[source, b], 0.0)
        out[:, b * q_blk : (b + 1) * q_blk] = track

    all_rs.wait_send()
    all_z.wait_send()
    ag_of(0).wait_send()
    ag_of(1).wait_send()
    on_chip.wait_send()
    for slot in range(3):
        for copy in part_copies(slot, sib, slot):
            copy.wait_send()
    halo(0).wait_send()
    halo(1).wait_send()
    for r in range(1, n_tm):

        @pl.when(t + r < n_tm)
        def _():
            terms_of(0, n_sp, r).wait_send()


def solution(mesh):
    n_tm, n_sp = mesh.shape["tm"], mesh.shape["space"]

    def local(fm, q_frame, q_row, q_col, decay, taps, pw, out_w):
        frames, rows, width, ch = fm.shape
        n_q = q_frame.shape[0]
        n_pos = rows * width
        plane = 2 * n_sp
        n_z = n_tm // 2
        home = n_q // plane
        q_blk = n_q // n_sp
        half = n_q // 2
        dims = (n_tm, n_sp, n_q, rows, width, ch, rows * n_sp)
        vmem = pl.BlockSpec(memory_space=pltpu.VMEM)
        dma = pltpu.SemaphoreType.DMA
        queries = [a.reshape(n_q // 128, 128) for a in (q_frame, q_row, q_col)]
        out = pl.pallas_call(
            functools.partial(kernel, dims),
            out_shape=pltpu.VMEM((2, n_q), F32),
            in_specs=[pl.BlockSpec(memory_space=pl.ANY)] * 8,
            out_specs=vmem,
            scratch_shapes=[
                pltpu.VMEM((3, n_q // 128, 128), jnp.int32),
                pltpu.VMEM(decay.shape, F32),
                pltpu.VMEM(taps.shape, F32),
                pltpu.VMEM(pw.shape, BF16),
                pltpu.VMEM(out_w.shape, F32),
                pltpu.VMEM((n_q // 128, 128), jnp.int32),
                pltpu.SMEM((n_q // 128, 128), jnp.int32),
                pltpu.VMEM((n_pos, ch), BF16),
                pltpu.VMEM((n_pos + 8, ch), F32),
                pltpu.VMEM((ch + 16, n_pos), BF16),
                pltpu.VMEM((n_q, ch), F32),
                pltpu.VMEM((plane, home, ch), BF16),
                pltpu.VMEM((plane - 1, home, ch), BF16),
                pltpu.VMEM((home, ch), BF16),
                pltpu.VMEM((n_z - 1, home, ch), BF16),
                pltpu.VMEM((home, ch), BF16),
                pltpu.VMEM((plane, home, ch), BF16),
                pltpu.VMEM((ch, half), BF16),
                pltpu.VMEM((ch, q_blk), BF16),
                pltpu.VMEM((n_tm, 1, ch), F32),
                pltpu.VMEM((3, ch, q_blk), F32),
                pltpu.VMEM((ch, ch), BF16),
                pltpu.VMEM((n_tm, 2, ch), F32),
                pltpu.VMEM((n_pos, half), F32),
                pltpu.VMEM((n_pos, q_blk), F32),
                pltpu.VMEM((ch + 16, half), F32),
                pltpu.VMEM((ch + 16, q_blk), F32),
                pltpu.VMEM((ch + 8, q_blk), F32),
                pltpu.VMEM((3, ch, q_blk), BF16),
                pltpu.VMEM((3, ch, q_blk), BF16),
                pltpu.VMEM((3, 8, q_blk), F32),
                pltpu.VMEM((3, 8, q_blk), F32),
                pltpu.VMEM((ch, q_blk), BF16),
                pltpu.VMEM((2, ch, q_blk), BF16),
                pltpu.VMEM((n_tm, 2, q_blk), F32),
                pltpu.VMEM((n_tm, n_sp, 2, q_blk), F32),
                dma((3,)), dma((4,)), dma((4,)), dma, dma, dma, dma, dma, dma((2,)), dma((2,)), dma, dma, dma, dma,
                dma((3,)), dma((3,)), dma((3,)), dma((3,)), dma((2,)), dma((2,)),
                dma((n_tm,)), dma((n_tm,)),
            ],
            compiler_params=pltpu.CompilerParams(collective_id=0, has_side_effects=True),
        )(fm.reshape(n_pos, ch), *queries, decay, taps, pw, out_w)
        return out[None]

    placed = (
        P(("video", "tm"), "space", None, None),
        P("video"),
        P("video"),
        P("video"),
        P(("video", "tm"), None),
        P(),
        P(),
        P(),
    )
    return jax.shard_map(
        local, mesh=mesh, in_specs=placed, out_specs=P(("video", "tm"), None, None), check_vma=False
    )
```

```python
import functools
import math

import jax
import jax.numpy as jnp
from jax import lax
from jax.experimental import pallas as pl
from jax.experimental.pallas import tpu as pltpu
from jax.sharding import PartitionSpec as P

MESH = pl.DeviceIdType.MESH
F32 = jnp.float32
BF16 = jnp.bfloat16


def far_first(n):
    return sorted(range(1, n), key=lambda r: -min(r, n - r))


def kernel(
    dims, fm, q_frame, q_row, q_col, decay_hbm, taps_hbm, pw_hbm, out_w_hbm, out,
    asked, decay, taps, pw, out_w, rows_v, rows_s, keys, keys32, keys_t, contrib32, contrib, rs_in, z_own, z_in, q_own, q_all, q_far, q_near, decay_all,
    tap_cols, pw_t, proj, even, odd, acc_far, acc, own_part, feats, feats_in, facts, facts_in, att_own, att_in, term, term_in,
    ask_sem, small_sem, key_sem, row_sem, rs_send, rs_recv, z_send, z_recv, ag_send, ag_recv, on_send,
    on_recv, dec_send, dec_recv,
    feat_send, feat_recv, fact_send, fact_recv, halo_send, halo_recv, term_send, term_recv,
):
    n_tm, n_sp, n_q, rows, width, ch, height = dims
    n_z = n_tm // 2
    plane = 2 * n_sp
    q_blk = n_q // n_sp
    n_pos = rows * width
    t = lax.axis_index("tm")
    y = lax.axis_index("space")
    z = lax.div(t, 2)
    core = lax.rem(t, 2)
    me = y * 2 + core

    def in_plane(r):
        other = lax.rem(me + r, plane)
        return other, {"tm": z * 2 + lax.rem(other, 2), "space": lax.div(other, 2)}

    def along_z(r):
        return {"tm": lax.rem(t + 2 * r, n_tm)}

    n_loads = 4
    piece = n_pos // n_loads

    def load(i):
        cut = pl.ds(i * piece, piece)
        return pltpu.make_async_copy(fm.at[cut], keys.at[cut], key_sem.at[i])

    asks = [
        pltpu.make_async_copy(a, asked.at[i], ask_sem.at[i])
        for i, a in enumerate([q_frame, q_row, q_col])
    ]
    smalls = [
        pltpu.make_async_copy(a, b, small_sem.at[i])
        for i, (a, b) in enumerate(
            [(decay_hbm, decay), (taps_hbm, taps), (pw_hbm, pw), (out_w_hbm, out_w)]
        )
    ]
    for copy in asks:
        copy.start()
    for i in range(n_loads):
        load(i).start()
    for copy in smalls:
        copy.start()
    barrier = pltpu.get_barrier_semaphore()
    for r in range(1, n_tm):
        pl.semaphore_signal(
            barrier, inc=1, device_id={"tm": lax.rem(t + r, n_tm)}, device_id_type=MESH
        )
    for r in range(1, n_sp):
        for c in range(2):
            pl.semaphore_signal(
                barrier, inc=1, device_id={"tm": z * 2 + c, "space": lax.rem(y + r, n_sp)},
                device_id_type=MESH,
            )
    for copy in asks:
        copy.wait()
    line = asked[0] * height + asked[1] - (t * height + y * rows)
    mine = (line >= 0) & (line < rows)
    rows_v[...] = jnp.where(mine, line * width + asked[2], n_pos)
    tell = pltpu.make_async_copy(rows_v, rows_s, row_sem)
    tell.start()
    step = 384
    keys32[pl.ds(n_pos, 8), :] = jnp.zeros((8, ch), F32)
    for i in range(n_loads):
        load(i).wait()

        @pl.loop(0, piece // step)
        def _(j):
            at = pl.multiple_of(i * piece + j * step, step)
            keys32[pl.ds(at, step), :] = keys[pl.ds(at, step), :].astype(F32)

    tell.wait()
    homes = plane // n_sp

    def rs_sends(k):
        for c in range(homes):
            block = lax.rem(y + k, n_sp)
            there = lax.rem(2 * (n_sp - k) + core - c + plane, plane) - 1

            @pl.when(there >= 0)
            def _():
                pltpu.make_async_remote_copy(
                    contrib.at[block * 2 + c], rs_in.at[there], rs_send, rs_recv,
                    device_id={"tm": z * 2 + c, "space": block}, device_id_type=MESH,
                ).start()

    @pl.loop(0, n_sp)
    def _(i):
        k = jnp.where(i == 0, 2, jnp.where(i == 1, 1, jnp.where(i == 2, 3, 0)))
        block = lax.rem(y + k, n_sp)
        first = pl.multiple_of(block * q_blk, q_blk)
        for u in range(q_blk):
            at = rows_s[block, u]
            contrib32[pl.ds(first + u, 1), :] = keys32[pl.ds(at, 1), :]
        contrib[pl.ds(block * 2, 2)] = (
            contrib32[pl.ds(first, q_blk), :].reshape(2, q_blk // 2, ch).astype(BF16)
        )

    pl.semaphore_wait(barrier, n_tm - 1 + plane - 2)
    for k in far_first(n_sp) + [0]:
        rs_sends(k)

    for copy in smalls:
        copy.wait()
    decay_all[t] = decay[...]

    @pl.loop(1, n_tm)
    def _(r):
        pltpu.make_async_remote_copy(
            decay, decay_all.at[t], dec_send, dec_recv,
            device_id={"tm": lax.rem(t + r, n_tm)}, device_id_type=MESH,
        ).start()

    all_rs = pltpu.make_async_remote_copy(
        rs_in, rs_in, rs_send, rs_recv, device_id=in_plane(1)[1], device_id_type=MESH
    )
    all_rs.wait_recv()
    total = contrib[me].astype(F32) + jnp.sum(rs_in[...].astype(F32), axis=0)
    z_own[...] = total.astype(BF16)
    for r in far_first(n_z):
        pltpu.make_async_remote_copy(
            z_own, z_in.at[r - 1], z_send, z_recv, device_id=along_z(r), device_id_type=MESH
        ).start()

    @pl.loop(0, n_pos // 128)
    def _(j):
        at = pl.multiple_of(j * 128, 128)
        keys_t[pl.ds(0, ch), pl.ds(at, 128)] = keys32[pl.ds(at, 128), :].T.astype(BF16)

    place = lax.broadcasted_iota(jnp.int32, (16, n_pos), 1).astype(F32)
    line = jnp.floor((place + 0.5) * (1.0 / width))
    col = place - line * width
    line = line + (y * rows).astype(F32)
    kind = lax.broadcasted_iota(jnp.int32, (16, n_pos), 0)
    extra = jnp.where(kind == 0, 1.0, jnp.where(kind == 1, col, jnp.where(kind == 2, line, 0.0)))
    keys_t[pl.ds(ch, 16), :] = extra.astype(BF16)

    all_z = pltpu.make_async_remote_copy(
        z_in, z_in, z_send, z_recv, device_id=along_z(1), device_id_type=MESH
    )
    all_z.wait_recv()
    total = total + jnp.sum(z_in[...].astype(F32), axis=0)
    q_own[...] = total.astype(BF16)
    q_all[me] = total.astype(BF16)
    on_chip = pltpu.make_async_remote_copy(
        q_own, q_all.at[me], on_send, on_recv, device_id={"tm": t + 1 - 2 * core},
        device_id_type=MESH,
    )
    on_chip.start()
    for k in (1, 3, 2):
        for c in range(2):
            pltpu.make_async_remote_copy(
                q_own, q_all.at[me], ag_send.at[k % 2], ag_recv.at[k % 2],
                device_id={"tm": z * 2 + c, "space": lax.rem(y + k, n_sp)}, device_id_type=MESH,
            ).start()

    odd_row = lax.rem(y, 2)
    scale = math.log2(math.e) / math.sqrt(ch)

    def turned(first, count):
        return q_all[pl.ds(first, count)].astype(F32).reshape(-1, ch).T.astype(BF16)

    def score(buf, q, at, size):
        s = jnp.dot(keys[pl.ds(at, size), :], q[...], preferred_element_type=F32)
        buf[pl.ds(at, size), :] = s
        return jnp.max(s.reshape(size // 8, 8, s.shape[1]), axis=0)

    def weigh(buf, total, at, size, top):
        e = jnp.exp2((buf[pl.ds(at, size), :] - top) * scale).astype(BF16)
        total[...] += jnp.dot(keys_t[:, pl.ds(at, size)], e, preferred_element_type=F32)

    step_both, step_last = n_pos // 3, n_pos // 2

    on_chip.wait_recv()
    q_near[...] = turned(2 * y, 2)
    top_own = jnp.max(score(odd, q_near, 0, n_pos), axis=0, keepdims=True)
    acc[...] = jnp.zeros_like(acc)

    @pl.loop(0, 2)
    def _(j):
        weigh(odd, acc, pl.multiple_of(j * step_last, step_last), step_last, top_own)

    own_part[...] = acc[pl.ds(0, ch + 8), :]

    eye = lax.broadcasted_iota(jnp.int32, (ch, ch), 0) == lax.broadcasted_iota(
        jnp.int32, (ch, ch), 1
    )
    for k in range(3):
        column = jnp.sum(jnp.where(eye, taps[pl.ds(k, 1), :], 0.0), axis=1, keepdims=True)
        tap_cols[k] = jnp.broadcast_to(column, (ch, q_blk))
    pw_t[...] = pw[...].astype(F32).T.astype(BF16)
    all_dec = pltpu.make_async_remote_copy(
        decay_all.at[pl.ds(0, n_tm - 1)], decay_all.at[pl.ds(0, n_tm - 1)], dec_send, dec_recv,
        device_id={"tm": lax.rem(t + 1, n_tm)}, device_id_type=MESH,
    )
    all_dec.wait()
    run = out_w[...] * (1.0 - decay[...])
    gain = jnp.zeros_like(run)
    for frame in range(n_tm):
        kept = gain if frame == 0 else gain * decay_all[frame]
        gain = jnp.where(t == frame, run, jnp.where(t < frame, kept, 0.0))
        proj[frame] = gain

    def ag_of(k):
        some = q_all.at[pl.ds(0, 2 + 2 * k)]
        return pltpu.make_async_remote_copy(
            some, some, ag_send.at[k], ag_recv.at[k],
            device_id=in_plane(1)[1], device_id_type=MESH,
        )

    ag_of(1).wait_recv()
    sib = lax.rem(y + 2, n_sp)
    for side in range(2):
        lanes = slice(side * q_blk, (side + 1) * q_blk)
        q_far[:, lanes] = turned(2 * (1 - odd_row) + 4 * side, 2)
    top_far = jnp.max(score(even, q_far, 0, n_pos), axis=0, keepdims=True)
    acc_far[...] = jnp.zeros_like(acc_far)
    ag_of(0).wait_recv()
    q_near[...] = turned(2 * sib, 2)

    def both(j, top):
        at = pl.multiple_of(j * step_both, step_both)
        top = jnp.maximum(top, score(odd, q_near, at, step_both))
        weigh(even, acc_far, at, step_both, top_far)
        return top

    top_sib = lax.fori_loop(0, 3, both, jnp.full((8, q_blk), -jnp.inf, F32))
    top_sib = jnp.max(top_sib, axis=0, keepdims=True)

    def hand_over(slot, to, there, sums, top):
        most = jnp.max(jnp.abs(sums[:ch]), axis=0, keepdims=True)
        grain = jnp.maximum(most, 1e-30) * (1.0 / 32000.0)
        feats[slot] = jnp.round(sums[:ch] * (1.0 / grain)).astype(jnp.int32).astype(jnp.int16)
        spare = lax.broadcasted_iota(jnp.int32, (8, q_blk), 0) == 3
        spare_2 = lax.broadcasted_iota(jnp.int32, (8, q_blk), 0) == 4
        facts[slot] = jnp.where(spare, top, jnp.where(spare_2, grain, sums[ch:]))
        for copy in part_copies(slot, to, there):
            copy.start()

    def part_copies(slot, to, there):
        return [
            pltpu.make_async_remote_copy(
                source.at[slot], target.at[there], send.at[slot], recv.at[there],
                device_id={"space": to}, device_id_type=MESH,
            )
            for source, target, send, recv in [
                (facts, facts_in, fact_send, fact_recv), (feats, feats_in, feat_send, feat_recv)
            ]
        ]

    for side in range(2):
        lanes = slice(side * q_blk, (side + 1) * q_blk)
        hand_over(
            side, 1 - odd_row + 2 * side, lax.div(y, 2), acc_far[pl.ds(0, ch + 8), lanes],
            top_far[:, lanes],
        )
    acc[...] = jnp.zeros_like(acc)

    @pl.loop(0, 2)
    def _(j):
        weigh(odd, acc, pl.multiple_of(j * step_last, step_last), step_last, top_sib)

    hand_over(2, sib, 2, acc[pl.ds(0, ch + 8), :], top_sib)
    parts = [(own_part[...], top_own)]
    for slot in range(3):
        for copy in part_copies(slot, sib, slot):
            copy.wait_recv()
    for slot in range(3):
        sums = jnp.concatenate([feats_in[slot].astype(jnp.int32).astype(F32) * facts_in[slot, pl.ds(4, 1), :], facts_in[slot]], axis=0)
        parts.append((sums, facts_in[slot, pl.ds(3, 1), :]))
    best = functools.reduce(jnp.maximum, [top for _, top in parts])
    mixed = None
    for sums, top in parts:
        v = sums * jnp.exp2((top - best) * scale)
        mixed = v if mixed is None else mixed + v
    inverse = 1.0 / mixed[ch : ch + 1]
    position = mixed[ch + 1 : ch + 3] * inverse
    unit = jnp.where(
        lax.broadcasted_iota(jnp.int32, (2, q_blk), 0) == 0, 1.0 / width, 1.0 / height
    )
    position = position * unit
    att = (mixed[:ch] * inverse).astype(BF16)
    att_own[...] = att

    def halo(side):
        to = lax.rem(t + (1 if side == 0 else n_tm - 1), n_tm)
        return pltpu.make_async_remote_copy(
            att_own, att_in.at[side], halo_send.at[side], halo_recv.at[side],
            device_id={"tm": to}, device_id_type=MESH,
        )

    halo(0).start()
    halo(1).start()
    att = att.astype(F32)
    mid = att * tap_cols[1]
    halo(0).wait_recv()
    halo(1).wait_recv()
    before = jnp.where(t > 0, att_in[0].astype(F32), 0.0)
    after = jnp.where(t < n_tm - 1, att_in[1].astype(F32), 0.0)
    depth = tap_cols[0] * before + mid + tap_cols[2] * after
    hidden = jax.nn.gelu(depth).astype(BF16)
    refined = att + jnp.dot(pw_t[...], hidden, preferred_element_type=F32)
    terms = jnp.dot(
        proj[...].reshape(2 * n_tm, ch), refined, preferred_element_type=F32,
        precision=lax.Precision.HIGHEST,
    )
    term[...] = terms.reshape(n_tm, 2, q_blk)

    own = term[t] + position
    term[t] = own
    term_in[t, y] = own

    def term_copy(r, k):
        return pltpu.make_async_remote_copy(
            term.at[t + r], term_in.at[t, y], term_send.at[r], term_recv.at[t],
            device_id={"tm": t + r, "space": lax.rem(y + k, n_sp)}, device_id_type=MESH,
        )

    def terms_of(source, count, slot):
        some = term_in.at[source, pl.ds(0, count)]
        return pltpu.make_async_remote_copy(
            some, some, term_send.at[slot], term_recv.at[source],
            device_id={"space": lax.rem(y + 1, n_sp)}, device_id_type=MESH,
        )

    for k in range(1, n_sp):
        term_copy(0, k).start()
    for r in range(1, n_tm):

        @pl.when(t + r < n_tm)
        def _():
            for k in range(n_sp):
                term_copy(r, k).start()

    for source in range(n_tm - 1):

        @pl.when(source < t)
        def _():
            terms_of(source, n_sp, 0).wait_recv()

    terms_of(t, n_sp - 1, 0).wait()
    for b in range(n_sp):
        track = term_in[t, b]
        for source in range(n_tm - 1):
            track = track + jnp.where(source < t, term_in[source, b], 0.0)
        out[:, b * q_blk : (b + 1) * q_blk] = track

    all_rs.wait_send()
    all_z.wait_send()
    ag_of(0).wait_send()
    ag_of(1).wait_send()
    on_chip.wait_send()
    for slot in range(3):
        for copy in part_copies(slot, sib, slot):
            copy.wait_send()
    halo(0).wait_send()
    halo(1).wait_send()
    for r in range(1, n_tm):

        @pl.when(t + r < n_tm)
        def _():
            terms_of(0, n_sp, r).wait_send()


def solution(mesh):
    n_tm, n_sp = mesh.shape["tm"], mesh.shape["space"]

    def local(fm, q_frame, q_row, q_col, decay, taps, pw, out_w):
        frames, rows, width, ch = fm.shape
        n_q = q_frame.shape[0]
        n_pos = rows * width
        plane = 2 * n_sp
        n_z = n_tm // 2
        home = n_q // plane
        q_blk = n_q // n_sp
        half = n_q // 2
        dims = (n_tm, n_sp, n_q, rows, width, ch, rows * n_sp)
        vmem = pl.BlockSpec(memory_space=pltpu.VMEM)
        dma = pltpu.SemaphoreType.DMA
        queries = [a.reshape(n_q // 128, 128) for a in (q_frame, q_row, q_col)]
        out = pl.pallas_call(
            functools.partial(kernel, dims),
            out_shape=pltpu.VMEM((2, n_q), F32),
            in_specs=[pl.BlockSpec(memory_space=pl.ANY)] * 8,
            out_specs=vmem,
            scratch_shapes=[
                pltpu.VMEM((3, n_q // 128, 128), jnp.int32),
                pltpu.VMEM(decay.shape, F32),
                pltpu.VMEM(taps.shape, F32),
                pltpu.VMEM(pw.shape, BF16),
                pltpu.VMEM(out_w.shape, F32),
                pltpu.VMEM((n_q // 128, 128), jnp.int32),
                pltpu.SMEM((n_q // 128, 128), jnp.int32),
                pltpu.VMEM((n_pos, ch), BF16),
                pltpu.VMEM((n_pos + 8, ch), F32),
                pltpu.VMEM((ch + 16, n_pos), BF16),
                pltpu.VMEM((n_q, ch), F32),
                pltpu.VMEM((plane, home, ch), BF16),
                pltpu.VMEM((plane - 1, home, ch), BF16),
                pltpu.VMEM((home, ch), BF16),
                pltpu.VMEM((n_z - 1, home, ch), BF16),
                pltpu.VMEM((home, ch), BF16),
                pltpu.VMEM((plane, home, ch), BF16),
                pltpu.VMEM((ch, half), BF16),
                pltpu.VMEM((ch, q_blk), BF16),
                pltpu.VMEM((n_tm, 1, ch), F32),
                pltpu.VMEM((3, ch, q_blk), F32),
                pltpu.VMEM((ch, ch), BF16),
                pltpu.VMEM((n_tm, 2, ch), F32),
                pltpu.VMEM((n_pos, half), F32),
                pltpu.VMEM((n_pos, q_blk), F32),
                pltpu.VMEM((ch + 16, half), F32),
                pltpu.VMEM((ch + 16, q_blk), F32),
                pltpu.VMEM((ch + 8, q_blk), F32),
                pltpu.VMEM((3, ch, q_blk), jnp.int16),
                pltpu.VMEM((3, ch, q_blk), jnp.int16),
                pltpu.VMEM((3, 8, q_blk), F32),
                pltpu.VMEM((3, 8, q_blk), F32),
                pltpu.VMEM((ch, q_blk), BF16),
                pltpu.VMEM((2, ch, q_blk), BF16),
                pltpu.VMEM((n_tm, 2, q_blk), F32),
                pltpu.VMEM((n_tm, n_sp, 2, q_blk), F32),
                dma((3,)), dma((4,)), dma((4,)), dma, dma, dma, dma, dma, dma((2,)), dma((2,)), dma, dma, dma, dma,
                dma((3,)), dma((3,)), dma((3,)), dma((3,)), dma((2,)), dma((2,)),
                dma((n_tm,)), dma((n_tm,)),
            ],
            compiler_params=pltpu.CompilerParams(collective_id=0, has_side_effects=True),
        )(fm.reshape(n_pos, ch), *queries, decay, taps, pw, out_w)
        return out[None]

    placed = (
        P(("video", "tm"), "space", None, None),
        P("video"),
        P("video"),
        P("video"),
        P(("video", "tm"), None),
        P(),
        P(),
        P(),
    )
    return jax.shard_map(
        local, mesh=mesh, in_specs=placed, out_specs=P(("video", "tm"), None, None), check_vma=False
    )
```

```python
import functools
import math

import jax
import jax.numpy as jnp
from jax import lax
from jax.experimental import pallas as pl
from jax.experimental.pallas import tpu as pltpu
from jax.sharding import PartitionSpec as P

MESH = pl.DeviceIdType.MESH
F32 = jnp.float32
BF16 = jnp.bfloat16


def far_first(n):
    return sorted(range(1, n), key=lambda r: -min(r, n - r))


def kernel(
    dims, fm, q_frame, q_row, q_col, decay_hbm, taps_hbm, pw_hbm, out_w_hbm, out,
    asked, decay, taps, pw, out_w, rows_v, rows_s, keys, keys32, keys_t, contrib32, contrib, rs_in, z_own, z_in, q_own, q_all, q_far, q_near, decay_all,
    tap_cols, pw_t, proj, even, odd, acc_far, acc, own_part, feats, feats_in, facts, facts_in, att_own, att_in, term, term_in,
    ask_sem, small_sem, key_sem, row_sem, rs_send, rs_recv, z_send, z_recv, ag_send, ag_recv, on_send,
    on_recv, dec_send, dec_recv,
    feat_send, feat_recv, fact_send, fact_recv, halo_send, halo_recv, term_send, term_recv,
):
    n_tm, n_sp, n_q, rows, width, ch, height = dims
    n_z = n_tm // 2
    plane = 2 * n_sp
    q_blk = n_q // n_sp
    n_pos = rows * width
    t = lax.axis_index("tm")
    y = lax.axis_index("space")
    z = lax.div(t, 2)
    core = lax.rem(t, 2)
    me = y * 2 + core

    def in_plane(r):
        other = lax.rem(me + r, plane)
        return other, {"tm": z * 2 + lax.rem(other, 2), "space": lax.div(other, 2)}

    def along_z(r):
        return {"tm": lax.rem(t + 2 * r, n_tm)}

    n_loads = 4
    piece = n_pos // n_loads

    def load(i):
        cut = pl.ds(i * piece, piece)
        return pltpu.make_async_copy(fm.at[cut], keys.at[cut], key_sem.at[i])

    asks = [
        pltpu.make_async_copy(a, asked.at[i], ask_sem.at[i])
        for i, a in enumerate([q_frame, q_row, q_col])
    ]
    smalls = [
        pltpu.make_async_copy(a, b, small_sem.at[i])
        for i, (a, b) in enumerate(
            [(decay_hbm, decay), (taps_hbm, taps), (pw_hbm, pw), (out_w_hbm, out_w)]
        )
    ]
    for copy in asks:
        copy.start()
    for i in range(n_loads):
        load(i).start()
    for copy in smalls:
        copy.start()
    barrier = pltpu.get_barrier_semaphore()
    for r in range(1, n_tm):
        pl.semaphore_signal(
            barrier, inc=1, device_id={"tm": lax.rem(t + r, n_tm)}, device_id_type=MESH
        )
    for r in range(1, n_sp):
        for c in range(2):
            pl.semaphore_signal(
                barrier, inc=1, device_id={"tm": z * 2 + c, "space": lax.rem(y + r, n_sp)},
                device_id_type=MESH,
            )
    for copy in asks:
        copy.wait()
    line = asked[0] * height + asked[1] - (t * height + y * rows)
    mine = (line >= 0) & (line < rows)
    rows_v[...] = jnp.where(mine, line * width + asked[2], n_pos)
    tell = pltpu.make_async_copy(rows_v, rows_s, row_sem)
    tell.start()
    step = 384
    keys32[pl.ds(n_pos, 8), :] = jnp.zeros((8, ch), F32)
    for i in range(n_loads):
        load(i).wait()

        @pl.loop(0, piece // step)
        def _(j):
            at = pl.multiple_of(i * piece + j * step, step)
            keys32[pl.ds(at, step), :] = keys[pl.ds(at, step), :].astype(F32)

    tell.wait()
    homes = plane // n_sp

    def rs_sends(k):
        for c in range(homes):
            block = lax.rem(y + k, n_sp)
            there = lax.rem(2 * (n_sp - k) + core - c + plane, plane) - 1

            @pl.when(there >= 0)
            def _():
                pltpu.make_async_remote_copy(
                    contrib.at[block * 2 + c], rs_in.at[there], rs_send, rs_recv,
                    device_id={"tm": z * 2 + c, "space": block}, device_id_type=MESH,
                ).start()

    @pl.loop(0, n_sp)
    def _(i):
        k = jnp.where(i == 0, 2, jnp.where(i == 1, 1, jnp.where(i == 2, 3, 0)))
        block = lax.rem(y + k, n_sp)
        first = pl.multiple_of(block * q_blk, q_blk)
        for u in range(q_blk):
            at = rows_s[block, u]
            contrib32[pl.ds(first + u, 1), :] = keys32[pl.ds(at, 1), :]
        contrib[pl.ds(block * 2, 2)] = (
            contrib32[pl.ds(first, q_blk), :].reshape(2, q_blk // 2, ch).astype(BF16)
        )

    pl.semaphore_wait(barrier, n_tm - 1 + plane - 2)
    for k in far_first(n_sp) + [0]:
        rs_sends(k)

    for copy in smalls:
        copy.wait()
    decay_all[t] = decay[...]

    @pl.loop(1, n_tm)
    def _(r):
        pltpu.make_async_remote_copy(
            decay, decay_all.at[t], dec_send, dec_recv,
            device_id={"tm": lax.rem(t + r, n_tm)}, device_id_type=MESH,
        ).start()

    all_rs = pltpu.make_async_remote_copy(
        rs_in, rs_in, rs_send, rs_recv, device_id=in_plane(1)[1], device_id_type=MESH
    )
    all_rs.wait_recv()
    total = contrib[me].astype(F32) + jnp.sum(rs_in[...].astype(F32), axis=0)
    z_own[...] = total.astype(BF16)
    for r in far_first(n_z):
        pltpu.make_async_remote_copy(
            z_own, z_in.at[r - 1], z_send, z_recv, device_id=along_z(r), device_id_type=MESH
        ).start()

    @pl.loop(0, n_pos // 128)
    def _(j):
        at = pl.multiple_of(j * 128, 128)
        keys_t[pl.ds(0, ch), pl.ds(at, 128)] = keys32[pl.ds(at, 128), :].T.astype(BF16)

    place = lax.broadcasted_iota(jnp.int32, (16, n_pos), 1).astype(F32)
    line = jnp.floor((place + 0.5) * (1.0 / width))
    col = place - line * width
    line = line + (y * rows).astype(F32)
    kind = lax.broadcasted_iota(jnp.int32, (16, n_pos), 0)
    extra = jnp.where(kind == 0, 1.0, jnp.where(kind == 1, col, jnp.where(kind == 2, line, 0.0)))
    keys_t[pl.ds(ch, 16), :] = extra.astype(BF16)

    all_z = pltpu.make_async_remote_copy(
        z_in, z_in, z_send, z_recv, device_id=along_z(1), device_id_type=MESH
    )
    all_z.wait_recv()
    total = total + jnp.sum(z_in[...].astype(F32), axis=0)
    q_own[...] = total.astype(BF16)
    q_all[me] = total.astype(BF16)
    on_chip = pltpu.make_async_remote_copy(
        q_own, q_all.at[me], on_send, on_recv, device_id={"tm": t + 1 - 2 * core},
        device_id_type=MESH,
    )
    on_chip.start()
    for k in (1, 3, 2):
        for c in range(2):
            pltpu.make_async_remote_copy(
                q_own, q_all.at[me], ag_send.at[k % 2], ag_recv.at[k % 2],
                device_id={"tm": z * 2 + c, "space": lax.rem(y + k, n_sp)}, device_id_type=MESH,
            ).start()

    odd_row = lax.rem(y, 2)
    scale = math.log2(math.e) / math.sqrt(ch)

    def turned(first, count):
        return q_all[pl.ds(first, count)].astype(F32).reshape(-1, ch).T.astype(BF16)

    def score(buf, q, at, size):
        s = jnp.dot(keys[pl.ds(at, size), :], q[...], preferred_element_type=F32)
        buf[pl.ds(at, size), :] = s
        return jnp.max(s.reshape(size // 8, 8, s.shape[1]), axis=0)

    def weigh(buf, total, at, size, top):
        e = jnp.exp2((buf[pl.ds(at, size), :] - top) * scale).astype(BF16)
        total[...] += jnp.dot(keys_t[:, pl.ds(at, size)], e, preferred_element_type=F32)

    step_both, step_last = n_pos // 3, n_pos // 2

    on_chip.wait_recv()
    q_near[...] = turned(2 * y, 2)
    top_own = jnp.max(score(odd, q_near, 0, n_pos), axis=0, keepdims=True)
    acc[...] = jnp.zeros_like(acc)

    @pl.loop(0, 2)
    def _(j):
        weigh(odd, acc, pl.multiple_of(j * step_last, step_last), step_last, top_own)

    own_part[...] = acc[pl.ds(0, ch + 8), :]

    eye = lax.broadcasted_iota(jnp.int32, (ch, ch), 0) == lax.broadcasted_iota(
        jnp.int32, (ch, ch), 1
    )
    for k in range(3):
        column = jnp.sum(jnp.where(eye, taps[pl.ds(k, 1), :], 0.0), axis=1, keepdims=True)
        tap_cols[k] = jnp.broadcast_to(column, (ch, q_blk))
    pw_t[...] = pw[...].astype(F32).T.astype(BF16)
    all_dec = pltpu.make_async_remote_copy(
        decay_all.at[pl.ds(0, n_tm - 1)], decay_all.at[pl.ds(0, n_tm - 1)], dec_send, dec_recv,
        device_id={"tm": lax.rem(t + 1, n_tm)}, device_id_type=MESH,
    )
    all_dec.wait()
    run = out_w[...] * (1.0 - decay[...])
    gain = jnp.zeros_like(run)
    for frame in range(n_tm):
        kept = gain if frame == 0 else gain * decay_all[frame]
        gain = jnp.where(t == frame, run, jnp.where(t < frame, kept, 0.0))
        proj[frame] = gain

    def ag_of(k):
        some = q_all.at[pl.ds(0, 2 + 2 * k)]
        return pltpu.make_async_remote_copy(
            some, some, ag_send.at[k], ag_recv.at[k],
            device_id=in_plane(1)[1], device_id_type=MESH,
        )

    ag_of(1).wait_recv()
    sib = lax.rem(y + 2, n_sp)
    for side in range(2):
        lanes = slice(side * q_blk, (side + 1) * q_blk)
        q_far[:, lanes] = turned(2 * (1 - odd_row) + 4 * side, 2)
    top_far = jnp.max(score(even, q_far, 0, n_pos), axis=0, keepdims=True)
    acc_far[...] = jnp.zeros_like(acc_far)
    ag_of(0).wait_recv()
    q_near[...] = turned(2 * sib, 2)

    def both(j, top):
        at = pl.multiple_of(j * step_both, step_both)
        top = jnp.maximum(top, score(odd, q_near, at, step_both))
        weigh(even, acc_far, at, step_both, top_far)
        return top

    top_sib = lax.fori_loop(0, 3, both, jnp.full((8, q_blk), -jnp.inf, F32))
    top_sib = jnp.max(top_sib, axis=0, keepdims=True)

    def hand_over(slot, to, there, sums, top):
        most = jnp.max(jnp.abs(sums[:ch]), axis=0, keepdims=True)
        grain = jnp.maximum(most, 1e-30) * (1.0 / 32000.0)
        feats[slot] = jnp.round(sums[:ch] * (1.0 / grain)).astype(jnp.int32).astype(jnp.int16)
        spare = lax.broadcasted_iota(jnp.int32, (8, q_blk), 0) == 3
        spare_2 = lax.broadcasted_iota(jnp.int32, (8, q_blk), 0) == 4
        facts[slot] = jnp.where(spare, top, jnp.where(spare_2, grain, sums[ch:]))
        for copy in part_copies(slot, to, there):
            copy.start()

    def part_copies(slot, to, there):
        return [
            pltpu.make_async_remote_copy(
                source.at[slot], target.at[there], send.at[slot], recv.at[there],
                device_id={"space": to}, device_id_type=MESH,
            )
            for source, target, send, recv in [
                (facts, facts_in, fact_send, fact_recv), (feats, feats_in, feat_send, feat_recv)
            ]
        ]

    for side in range(2):
        lanes = slice(side * q_blk, (side + 1) * q_blk)
        hand_over(
            side, 1 - odd_row + 2 * side, lax.div(y, 2), acc_far[pl.ds(0, ch + 8), lanes],
            top_far[:, lanes],
        )
    acc[...] = jnp.zeros_like(acc)

    @pl.loop(0, 2)
    def _(j):
        weigh(odd, acc, pl.multiple_of(j * step_last, step_last), step_last, top_sib)

    hand_over(2, sib, 2, acc[pl.ds(0, ch + 8), :], top_sib)
    parts = [(own_part[...], top_own)]
    for slot in range(3):
        for copy in part_copies(slot, sib, slot):
            copy.wait_recv()
    for slot in range(3):
        sums = jnp.concatenate([feats_in[slot].astype(jnp.int32).astype(F32) * facts_in[slot, pl.ds(4, 1), :], facts_in[slot]], axis=0)
        parts.append((sums, facts_in[slot, pl.ds(3, 1), :]))
    best = functools.reduce(jnp.maximum, [top for _, top in parts])
    mixed = None
    for sums, top in parts:
        v = sums * jnp.exp2((top - best) * scale)
        mixed = v if mixed is None else mixed + v
    inverse = 1.0 / mixed[ch : ch + 1]
    position = mixed[ch + 1 : ch + 3] * inverse
    unit = jnp.where(
        lax.broadcasted_iota(jnp.int32, (2, q_blk), 0) == 0, 1.0 / width, 1.0 / height
    )
    position = position * unit
    att = (mixed[:ch] * inverse).astype(BF16)
    att_own[...] = att

    def halo(side):
        to = lax.rem(t + (1 if side == 0 else n_tm - 1), n_tm)
        return pltpu.make_async_remote_copy(
            att_own, att_in.at[side], halo_send.at[side], halo_recv.at[side],
            device_id={"tm": to}, device_id_type=MESH,
        )

    for side, there in ((0, t < n_tm - 1), (1, t > 0)):

        @pl.when(there)
        def _():
            halo(side).start()

    att = att.astype(F32)
    mid = att * tap_cols[1]
    for side, there in ((0, t > 0), (1, t < n_tm - 1)):

        @pl.when(there)
        def _():
            halo(side).wait_recv()

    before = jnp.where(t > 0, att_in[0].astype(F32), 0.0)
    after = jnp.where(t < n_tm - 1, att_in[1].astype(F32), 0.0)
    depth = tap_cols[0] * before + mid + tap_cols[2] * after
    hidden = jax.nn.gelu(depth).astype(BF16)
    refined = att + jnp.dot(pw_t[...], hidden, preferred_element_type=F32)
    terms = jnp.dot(
        proj[...].reshape(2 * n_tm, ch), refined, preferred_element_type=F32,
        precision=lax.Precision.HIGHEST,
    )
    term[...] = terms.reshape(n_tm, 2, q_blk)

    own = term[t] + position
    term[t] = own
    term_in[t, y] = own

    def term_copy(r, k):
        return pltpu.make_async_remote_copy(
            term.at[t + r], term_in.at[t, y], term_send.at[r], term_recv.at[t],
            device_id={"tm": t + r, "space": lax.rem(y + k, n_sp)}, device_id_type=MESH,
        )

    def terms_of(source, count, slot):
        some = term_in.at[source, pl.ds(0, count)]
        return pltpu.make_async_remote_copy(
            some, some, term_send.at[slot], term_recv.at[source],
            device_id={"space": lax.rem(y + 1, n_sp)}, device_id_type=MESH,
        )

    for k in range(1, n_sp):
        term_copy(0, k).start()
    for r in range(1, n_tm):

        @pl.when(t + r < n_tm)
        def _():
            for k in range(n_sp):
                term_copy(r, k).start()

    for source in range(n_tm - 1):

        @pl.when(source < t)
        def _():
            terms_of(source, n_sp, 0).wait_recv()

    terms_of(t, n_sp - 1, 0).wait()
    for b in range(n_sp):
        track = term_in[t, b]
        for source in range(n_tm - 1):
            track = track + jnp.where(source < t, term_in[source, b], 0.0)
        out[:, b * q_blk : (b + 1) * q_blk] = track

    all_rs.wait_send()
    all_z.wait_send()
    ag_of(0).wait_send()
    ag_of(1).wait_send()
    on_chip.wait_send()
    for slot in range(3):
        for copy in part_copies(slot, sib, slot):
            copy.wait_send()
    for side, there in ((0, t < n_tm - 1), (1, t > 0)):

        @pl.when(there)
        def _():
            halo(side).wait_send()

    for r in range(1, n_tm):

        @pl.when(t + r < n_tm)
        def _():
            terms_of(0, n_sp, r).wait_send()


def solution(mesh):
    n_tm, n_sp = mesh.shape["tm"], mesh.shape["space"]

    def local(fm, q_frame, q_row, q_col, decay, taps, pw, out_w):
        frames, rows, width, ch = fm.shape
        n_q = q_frame.shape[0]
        n_pos = rows * width
        plane = 2 * n_sp
        n_z = n_tm // 2
        home = n_q // plane
        q_blk = n_q // n_sp
        half = n_q // 2
        dims = (n_tm, n_sp, n_q, rows, width, ch, rows * n_sp)
        vmem = pl.BlockSpec(memory_space=pltpu.VMEM)
        dma = pltpu.SemaphoreType.DMA
        queries = [a.reshape(n_q // 128, 128) for a in (q_frame, q_row, q_col)]
        out = pl.pallas_call(
            functools.partial(kernel, dims),
            out_shape=pltpu.VMEM((2, n_q), F32),
            in_specs=[pl.BlockSpec(memory_space=pl.ANY)] * 8,
            out_specs=vmem,
            scratch_shapes=[
                pltpu.VMEM((3, n_q // 128, 128), jnp.int32),
                pltpu.VMEM(decay.shape, F32),
                pltpu.VMEM(taps.shape, F32),
                pltpu.VMEM(pw.shape, BF16),
                pltpu.VMEM(out_w.shape, F32),
                pltpu.VMEM((n_q // 128, 128), jnp.int32),
                pltpu.SMEM((n_q // 128, 128), jnp.int32),
                pltpu.VMEM((n_pos, ch), BF16),
                pltpu.VMEM((n_pos + 8, ch), F32),
                pltpu.VMEM((ch + 16, n_pos), BF16),
                pltpu.VMEM((n_q, ch), F32),
                pltpu.VMEM((plane, home, ch), BF16),
                pltpu.VMEM((plane - 1, home, ch), BF16),
                pltpu.VMEM((home, ch), BF16),
                pltpu.VMEM((n_z - 1, home, ch), BF16),
                pltpu.VMEM((home, ch), BF16),
                pltpu.VMEM((plane, home, ch), BF16),
                pltpu.VMEM((ch, half), BF16),
                pltpu.VMEM((ch, q_blk), BF16),
                pltpu.VMEM((n_tm, 1, ch), F32),
                pltpu.VMEM((3, ch, q_blk), F32),
                pltpu.VMEM((ch, ch), BF16),
                pltpu.VMEM((n_tm, 2, ch), F32),
                pltpu.VMEM((n_pos, half), F32),
                pltpu.VMEM((n_pos, q_blk), F32),
                pltpu.VMEM((ch + 16, half), F32),
                pltpu.VMEM((ch + 16, q_blk), F32),
                pltpu.VMEM((ch + 8, q_blk), F32),
                pltpu.VMEM((3, ch, q_blk), jnp.int16),
                pltpu.VMEM((3, ch, q_blk), jnp.int16),
                pltpu.VMEM((3, 8, q_blk), F32),
                pltpu.VMEM((3, 8, q_blk), F32),
                pltpu.VMEM((ch, q_blk), BF16),
                pltpu.VMEM((2, ch, q_blk), BF16),
                pltpu.VMEM((n_tm, 2, q_blk), F32),
                pltpu.VMEM((n_tm, n_sp, 2, q_blk), F32),
                dma((3,)), dma((4,)), dma((4,)), dma, dma, dma, dma, dma, dma((2,)), dma((2,)), dma, dma, dma, dma,
                dma((3,)), dma((3,)), dma((3,)), dma((3,)), dma((2,)), dma((2,)),
                dma((n_tm,)), dma((n_tm,)),
            ],
            compiler_params=pltpu.CompilerParams(collective_id=0, has_side_effects=True),
        )(fm.reshape(n_pos, ch), *queries, decay, taps, pw, out_w)
        return out[None]

    placed = (
        P(("video", "tm"), "space", None, None),
        P("video"),
        P("video"),
        P("video"),
        P(("video", "tm"), None),
        P(),
        P(),
        P(),
    )
    return jax.shard_map(
        local, mesh=mesh, in_specs=placed, out_specs=P(("video", "tm"), None, None), check_vma=False
    )
```
